128 devices in a mesh: feed: 16 (over z, y_hi, core), chan: 8 (over x, y_lo).
Axes of the slice: x: 4, y: 4 (y_hi: 2, y_lo: 2; y = y_hi * 2 + y_lo), z: 4, core: 2. Of those that a mesh axis runs over, the one named last changes fastest.
Arguments:
- raw_samples: bfloat16 [256, 90112], P(('feed', 'chan')), may hold values from -6 to 6
- stack_code: int32 [256, 256], P('feed'), may hold values from -382 to 381, as said below
- stack_owner: int32 [382], replicated, may hold values from 0 to 15, as said below
Outputs:
- visibilities: float32 [752, 2, 2048], P('feed', None, 'chan')
The draws below stay inside these ranges and needn't reach their ends.
Inputs may be any that keep to these rules, and one draw needn't show every extreme that they name: `stack_code`: entry [i, j] names the stack of the baseline from input i to input j: s when it has stack s's orientation, -1 - s when reversed. For i != j entry [j, i] is -1 minus entry [i, j]; the diagonal holds 0; every stack is named. `stack_owner`: no owner has more than 47 stacks, and one owner has exactly 47.
All inputs are finite; a program needn't handle non-finite values.
Results may differ from the reference program's by a relative error of at most 0.0083.
Values may be sent and summed in bfloat16 or wider, within the bound.
A program may use at most 64 MiB of HBM per device.

```python
import math
import jax
import jax.numpy as jnp
from jax import lax

NS = 128
INPUTS = 256
SPECTRA = 4
TAPS = 8
FA = 64
FB = 128
FRAME = 8192
CHANS = 2048
SAMPLES = 90112
STACKS = 382
OWNERS = 16
CAP = 47


def draw_stack_code(key, part):
    position = jax.random.permutation(jax.random.fold_in(key, 11), INPUTS).astype(jnp.int32)
    cylinder = position // NS
    along_ns = position % NS
    offset_east = cylinder[None, :] - cylinder[:, None]
    offset_north = along_ns[None, :] - along_ns[:, None]
    forward = (offset_east > 0) | (offset_east == 0) & (offset_north > 0)
    canon_east = jnp.where(forward, offset_east, -offset_east)
    canon_north = jnp.where(forward, offset_north, -offset_north)
    stack_id = jnp.where(canon_east == 0, canon_north - 1, NS - 1 + (canon_east - 1) * (2 * NS - 1) + canon_north + NS - 1)
    return jnp.where(forward, stack_id, -1 - stack_id).astype(jnp.int32)


def draw_stack_owner(key, part):
    shuffled = jax.random.permutation(jax.random.fold_in(key, 21), STACKS)
    busiest = jax.random.randint(jax.random.fold_in(key, 22), (), 0, OWNERS)
    remain = STACKS - CAP
    spacing = remain // (OWNERS - 1)
    jitter = jax.random.randint(jax.random.fold_in(key, 23), (OWNERS - 2,), -(spacing // 4), spacing // 4 + 1)
    bounds = jnp.arange(1, OWNERS - 1) * remain // (OWNERS - 1) + jitter
    ranked = jnp.arange(STACKS) - CAP
    group_id = jnp.sum((ranked[:, None] >= bounds[None, :]).astype(jnp.int32), axis=1)
    others = jnp.where(group_id >= busiest, group_id + 1, group_id)
    assigned = jnp.where(ranked < 0, busiest, others).astype(jnp.int32)
    return jnp.zeros((STACKS,), jnp.int32).at[shuffled].set(assigned)


def block_levels(stream_key, dims, cuts, least, top_value):
    def one(dim, blocks):
        draws = jax.random.uniform(jax.random.fold_in(jax.random.fold_in(stream_key, 6), dim), (blocks,), jnp.float32, least / len(cuts), top_value / len(cuts))
        return jnp.repeat(jnp.exp(draws), dims[dim] // blocks).reshape((-1,) + (1,) * (len(dims) - dim - 1))

    loudness = one(*cuts[0])
    for cut in cuts[1:]:
        loudness = loudness * one(*cut)
    return loudness


def gaussian(key, dims, width, bound, cuts=(), kind=jnp.bfloat16):
    level = block_levels(key, dims, cuts, -0.22, 0.18) if cuts else 1.0
    result = jax.random.normal(key, dims, jnp.float32) * width * level
    return jnp.minimum(jnp.maximum(result, -bound), bound).astype(kind)


def setup_inputs(seed: int = 0) -> dict:
    arg_keys = jax.random.split(jax.random.key(seed), 4)
    return {
        "raw_samples": gaussian(arg_keys[0], (INPUTS, SAMPLES), 1.0, 6.0, ((0, 128),)),
        "stack_code": draw_stack_code(jax.random.fold_in(arg_keys[3], 71), 0),
        "stack_owner": draw_stack_owner(jax.random.fold_in(arg_keys[3], 71), 0),
    }


def window_table():
    length = TAPS * FRAME
    sample = jnp.arange(length).astype(jnp.float32)
    centred = (sample - length / 2 + 0.5) / FRAME
    hanning = 0.5 - 0.5 * jnp.cos(2.0 * math.pi * (sample + 0.5) / length)
    weights = jnp.sinc(centred) * hanning
    weights = weights * jnp.sqrt(FRAME / jnp.sum(weights * weights))
    return weights.reshape(TAPS, FRAME)

def angle_of(left_index, right_index, modulus):
    product = left_index[:, None] * right_index[None, :] % modulus
    return 2.0 * math.pi * product.astype(jnp.float32) / modulus

def first_table():
    angles = angle_of(jnp.arange(FA, dtype=jnp.int32), jnp.arange(FA, dtype=jnp.int32), FA)
    return jnp.concatenate([jnp.cos(angles), -jnp.sin(angles)], axis=1).astype(jnp.bfloat16)

def twiddles():
    angles = angle_of(jnp.arange(FA, dtype=jnp.int32), jnp.arange(FB, dtype=jnp.int32), FRAME)
    return (jnp.cos(angles), jnp.sin(angles))

def second_table(second_count):
    angles = angle_of(jnp.arange(FB, dtype=jnp.int32), jnp.arange(second_count, dtype=jnp.int32), FB)
    cosine = jnp.cos(angles)
    sine_part = jnp.sin(angles)
    top_rows = jnp.stack([cosine, -sine_part], axis=1)
    low_rows = jnp.stack([sine_part, cosine], axis=1)
    return jnp.stack([top_rows, low_rows], axis=0).astype(jnp.bfloat16)

def channelize(samples, second_count):
    window = window_table()
    inputs = samples.shape[0]
    framed = samples.reshape(inputs, SPECTRA + TAPS - 1, FRAME)
    summed = jnp.zeros((inputs, SPECTRA, FRAME), jnp.float32)
    for tap_index in range(TAPS):
        summed = summed + window[tap_index] * framed[:, tap_index:tap_index + SPECTRA].astype(jnp.float32)
    frames = summed.astype(jnp.bfloat16).reshape(inputs * SPECTRA, FA, FB)
    sectioned = jnp.einsum('rab,ak->rkb', frames.astype(jnp.float32), first_table().astype(jnp.float32))
    cosine, sine_part = twiddles()
    real_part = sectioned[:, :FA]
    imag_part = sectioned[:, FA:]
    mixed = jnp.stack([real_part * cosine + imag_part * sine_part, imag_part * cosine - real_part * sine_part], axis=2)
    mixed = mixed.astype(jnp.bfloat16)
    spectra = jnp.einsum('rkpb,pbqm->rqmk', mixed.astype(jnp.float32), second_table(second_count).astype(jnp.float32))
    spectra = spectra / math.sqrt(FRAME)
    return spectra.reshape(inputs, SPECTRA, 2, second_count * FA).astype(jnp.bfloat16)

def correlate(own_block, other_block):
    left_rows = own_block.reshape(own_block.shape[0], 2 * own_block.shape[1], own_block.shape[3])
    turned = jnp.stack([-other_block[:, :, 1], other_block[:, :, 0]], axis=2)
    right_rows = jnp.stack([other_block, turned], axis=3)
    right_rows = right_rows.reshape(other_block.shape[0], 2 * other_block.shape[1], 2, other_block.shape[3])
    return jnp.einsum('ikc,jkqc->ijqc', left_rows.astype(jnp.float32), right_rows.astype(jnp.float32))

def stack_targets(code_rows, usable):
    target = jnp.where(code_rows >= 0, code_rows, -1 - code_rows)
    return jnp.where(usable, target, STACKS)

def add_pairs(totals, values, code_rows, usable):
    target = stack_targets(code_rows, usable)
    orient = jnp.where(code_rows >= 0, 1.0, -1.0).astype(jnp.float32)
    values = jnp.stack([values[:, :, 0], values[:, :, 1] * orient[:, :, None]], axis=2)
    flattened = values.reshape(-1, 2, values.shape[3])
    return totals + jax.ops.segment_sum(flattened, target.reshape(-1), num_segments=STACKS + 1)

def slot_sources(owner_ids, owners, capacity, stacks):
    member = (owner_ids[:, None] == jnp.arange(owners, dtype=jnp.int32)[None, :]).astype(jnp.int32)
    earlier = jnp.cumsum(member, axis=0) - member
    ranking = lax.optimization_barrier(jnp.sum(earlier * member, axis=1))
    slot_ids = owner_ids * capacity + ranking
    filled = jnp.full((owners * capacity,), stacks, jnp.int32)
    return filled.at[slot_ids].set(jnp.arange(stacks, dtype=jnp.int32))

def reference(raw_samples, stack_code, stack_owner):
    group_rows = min(64, INPUTS)
    groups = INPUTS // group_rows
    second_count = CHANS // FA

    def one_group(grouped):
        return channelize(grouped, second_count)
    spectra = lax.map(one_group, raw_samples.reshape(groups, group_rows, SAMPLES))
    local_ids = jnp.arange(group_rows, dtype=jnp.int32)
    empty = jnp.zeros((STACKS + 1, 2, CHANS), jnp.float32)

    def outer(totals, left_index):
        own = spectra[left_index]
        row_ids = left_index * group_rows + local_ids

        def inner(running, right_index):
            other = spectra[right_index]
            col_ids = right_index * group_rows + local_ids
            usable = col_ids[None, :] > row_ids[:, None]
            code_rows = lax.dynamic_slice(stack_code, (left_index * group_rows, right_index * group_rows), (group_rows, group_rows))
            return (add_pairs(running, correlate(own, other), code_rows, usable), None)
        return (lax.scan(inner, totals, jnp.arange(groups, dtype=jnp.int32))[0], None)
    totals = lax.scan(outer, empty, jnp.arange(groups, dtype=jnp.int32))[0]
    all_ids = jnp.arange(INPUTS, dtype=jnp.int32)
    upper = all_ids[None, :] > all_ids[:, None]
    target = stack_targets(stack_code, upper)
    counts = jax.ops.segment_sum(jnp.ones((INPUTS * INPUTS,), jnp.float32), target.reshape(-1), num_segments=STACKS + 1)
    means = totals / jnp.maximum(counts, 1.0)[:, None, None]
    means = means.at[STACKS].set(0.0)
    sources = slot_sources(stack_owner, OWNERS, CAP, STACKS)
    return means[sources]
```

```python
import math

import numpy as np
import jax
import jax.numpy as jnp
from jax import lax
from jax.experimental import pallas as pl
from jax.experimental.pallas import tpu as pltpu
from jax.sharding import PartitionSpec as P

SPECTRA = 4
TAPS = 8
FA = 64
FB = 128
FRAME = 8192
STACKS = 382
CAP = 47
FEEDS = 16
GROUPS = 8
INPUTS = 256
HALF = 128
CHUNK = 8
NB = 3
F32 = jnp.float32
BF16 = jnp.bfloat16
NT = (((1,), (1,)), ((), ()))


def window_table():
    length = TAPS * FRAME
    sample = np.arange(length, dtype=np.float64)
    centred = (sample - length / 2 + 0.5) / FRAME
    weights = np.sinc(centred) * (0.5 - 0.5 * np.cos(2.0 * np.pi * (sample + 0.5) / length))
    weights = weights * np.sqrt(FRAME / np.sum(weights * weights))
    return weights.reshape(TAPS, FA, FB).astype(np.float32)


def turns(left, right, modulus):
    return 2.0 * np.pi * (np.outer(left, right) % modulus) / modulus


def first_matrix():
    angles = turns(np.arange(FA), np.arange(FA), FA)
    parts = np.stack([np.cos(angles), -np.sin(angles)]).reshape(2, FA, 4, 16)
    out = np.zeros((2, 4, 2, 16, FA, 2), np.float32)
    for i in range(2):
        out[:, :, i, :, :, i] = parts.transpose(0, 2, 3, 1)
    return out.reshape(256, 128)


def twiddle_tables():
    angles = turns(np.arange(FA), np.arange(FB), FRAME).reshape(4, 1, 16, FB)
    angles = np.broadcast_to(angles, (4, 2, 16, FB)).reshape(128, FB)
    return np.stack([np.cos(angles), np.sin(angles)]).astype(np.float32)


def second_matrix():
    angles = turns(np.arange(32), np.arange(FB), FB)
    return np.concatenate([np.cos(angles), np.sin(angles)], axis=1).astype(np.float32)


def bf(table):
    return jnp.asarray(table).astype(BF16)


def channelize(x_ref, win_ref, first_ref, tw_ref, second_ref, mixed_ref, wide_ref):
    frames = []
    for t in range(SPECTRA):
        total = jnp.zeros((128, FB), F32)
        for p in range(TAPS):
            rows = x_ref[pl.ds((t + p) * 128, 128), :].astype(F32)
            total = total + win_ref[p] * rows
        frames.append(total.astype(BF16))
    frames = jnp.concatenate(frames, axis=1)
    section = jnp.dot(first_ref[...], frames, preferred_element_type=F32)
    cosine, sine = tw_ref[0], tw_ref[1]
    for t in range(SPECTRA):
        re = section[:128, t * FB : (t + 1) * FB]
        im = section[128:, t * FB : (t + 1) * FB]
        real = re * cosine + im * sine
        imag = im * cosine - re * sine
        minus = (-real).astype(BF16)
        real = real.astype(BF16)
        imag = imag.astype(BF16)
        for u in range(8):
            rows = slice(u * 16, u * 16 + 16)
            base = (u * 8 + t) * 16
            mixed_ref[base : base + 16, :FB] = real[rows]
            mixed_ref[base : base + 16, FB:] = imag[rows]
            base = (u * 8 + 4 + t) * 16
            mixed_ref[base : base + 16, :FB] = imag[rows]
            mixed_ref[base : base + 16, FB:] = minus[rows]
    out = lax.dot_general(second_ref[...], mixed_ref[...], NT, preferred_element_type=F32)
    out = out * (1.0 / math.sqrt(FRAME))
    for u in range(8):
        wide_ref[pl.ds(u, 32, stride=8), :] = out[:, u * 128 : (u + 1) * 128]
    return wide_ref[...].astype(BF16)


def regroup(block):
    row = lax.broadcasted_iota(jnp.int32, (256, 256), 0)
    col = lax.broadcasted_iota(jnp.int32, (256, 256), 1)
    source = ((row // 2) % 8) * 32 + (row // 16) * 2 + row % 2
    take = jnp.where(col == source, 1.0, 0.0).astype(BF16)
    return jnp.dot(take, block, preferred_element_type=F32).astype(BF16)


def stack_pairs(x_ref, code_ref, xf_ref, left_ref, right_ref, data_ref, hot_ref, acc_ref):
    x = x_ref[...]
    xf = x.astype(F32)
    xf_ref[0] = xf
    xf_ref[1] = jnp.concatenate([xf[:, 64:], -xf[:, :64]], axis=1)
    acc_ref[...] = jnp.zeros_like(acc_ref)
    lane = lax.broadcasted_iota(jnp.int32, (16, 128), 1)
    sub = lax.broadcasted_iota(jnp.int32, (16, 128), 0)
    pick = lane % 16 == sub
    hot_row = lax.broadcasted_iota(jnp.int32, (128, INPUTS), 0)
    lane_j = lax.broadcasted_iota(jnp.int32, (32, 128), 1)
    bid = lax.broadcasted_iota(jnp.int32, (16, INPUTS), 0)

    @pl.loop(0, HALF // CHUNK)
    def _(step):
        base = step * CHUNK
        for n in range(CHUNK):
            for q in range(2):
                at = slice(n * 32 + q * 16, n * 32 + q * 16 + 16)
                row = xf_ref[q, pl.ds(base + n, 1), :]
                left_ref[at, :] = jnp.where(pick, row, 0.0).astype(BF16)
                row = xf_ref[q, pl.ds(HALF + base + n, 1), :]
                right_ref[at, :] = jnp.where(pick, row, 0.0).astype(BF16)
        one = lax.dot_general(left_ref[...], x_ref[...], NT, preferred_element_type=F32)
        two = lax.dot_general(right_ref[...], x_ref[HALF:, :], NT, preferred_element_type=F32)
        for n in range(CHUNK):
            at = slice(n * 32, n * 32 + 32)
            low = jnp.where(lane_j > base + n, one[at, :128], two[at, :])
            both = jnp.concatenate([low, one[at, 128:]], axis=1)
            code = code_ref[pl.ds(base + n, 1), :]
            target = jnp.where(code >= 0, code, -1 - code)
            sign = jnp.where(code >= 0, 1.0, -1.0).astype(F32)
            used = lax.broadcasted_iota(jnp.int32, (1, INPUTS), 1) != base + n
            hi = target // 128
            lo = jnp.where(used, target % 128, -1)
            real = both[:16].astype(BF16)
            imag = (both[16:] * sign).astype(BF16)
            lanes = slice(n * INPUTS, (n + 1) * INPUTS)
            zero = jnp.zeros((), BF16)
            for b in range(NB):
                data_ref[b * 32 : b * 32 + 16, lanes] = jnp.where(hi == b, real, zero)
                data_ref[b * 32 + 16 : b * 32 + 32, lanes] = jnp.where(hi == b, imag, zero)
            data_ref[NB * 32 : NB * 32 + 16, lanes] = jnp.where(hi == bid, 1.0, 0.0).astype(BF16)
            hot_ref[:, lanes] = jnp.where(hot_row == lo, 1.0, 0.0).astype(BF16)
        acc_ref[...] += lax.dot_general(data_ref[...], hot_ref[...], NT, preferred_element_type=F32)


def messages(acc_ref, owner_ref):
    owner = owner_ref[...]
    wide = jnp.broadcast_to(owner, (128, NB * 128))
    tall = jnp.transpose(wide.astype(F32))
    rank = jnp.zeros((1, NB * 128), F32)
    cols = []
    for b in range(NB):
        mine = owner[:, b * 128 : (b + 1) * 128].astype(F32)
        row = lax.broadcasted_iota(jnp.int32, (NB * 128, 128), 0)
        col = lax.broadcasted_iota(jnp.int32, (NB * 128, 128), 1) + b * 128
        same = jnp.where((tall == mine) & (row < col), 1.0, 0.0)
        cols.append(jnp.sum(same, axis=0, keepdims=True))
    rank = jnp.concatenate(cols, axis=1).astype(jnp.int32)
    place = jnp.where(owner >= 0, owner * 128 + rank, -1)
    slot = lax.broadcasted_iota(jnp.int32, (FEEDS * 128, NB * 128), 0)
    perm_re = jnp.where(slot == place, 1.0, 0.0).astype(BF16)
    perm_im = jnp.where(slot == jnp.where(owner >= 0, place + 64, -1), 1.0, 0.0).astype(BF16)
    perm = jnp.concatenate([perm_re, perm_im], axis=1)
    parts = []
    for q in range(2):
        for b in range(NB):
            sums = acc_ref[b * 32 + q * 16 : b * 32 + q * 16 + 16, :]
            count = acc_ref[NB * 32 + b : NB * 32 + b + 1, :]
            parts.append(sums / jnp.maximum(count, 1.0))
    means = jnp.concatenate(parts, axis=1)
    high = means.astype(BF16)
    low = (means - high.astype(F32)).astype(BF16)
    both = jnp.concatenate([high, low], axis=0)
    out = lax.dot_general(both, perm, NT, preferred_element_type=F32)
    return out[:16] + out[16:]


def finish(block, out_ref):
    turned = jnp.transpose(block)
    out_ref[:, 0, :] = turned[:CAP]
    out_ref[:, 1, :] = turned[64 : 64 + CAP]


def k_channelize(x_ref, win_ref, first_ref, tw_ref, second_ref, out_ref, mixed_ref, wide_ref):
    out_ref[...] = channelize(x_ref, win_ref, first_ref, tw_ref, second_ref, mixed_ref, wide_ref)


def k_regroup(in_ref, out_ref):
    out_ref[...] = regroup(in_ref[...])


def k_stack(x_ref, code_ref, owner_ref, out_ref, xf, left, right, data, hot, acc):
    stack_pairs(x_ref, code_ref, xf, left, right, data, hot, acc)
    out = messages(acc, owner_ref)
    for o in range(FEEDS):
        out_ref[o] = out[:, o * 128 : (o + 1) * 128]


def k_finish(in_ref, out_ref):
    finish(in_ref[...], out_ref)


def call(kernel, shape, dtype, scratch, *args):
    return pl.pallas_call(
        kernel,
        out_shape=jax.ShapeDtypeStruct(shape, dtype),
        in_specs=[pl.BlockSpec(memory_space=pltpu.VMEM)] * len(args),
        out_specs=pl.BlockSpec(memory_space=pltpu.VMEM),
        scratch_shapes=scratch,
        compiler_params=pltpu.CompilerParams(vmem_limit_bytes=60 << 20),
    )(*args)


def fold_codes(codes):
    row = lax.broadcasted_iota(jnp.int32, (HALF, HALF), 0)
    col = lax.broadcasted_iota(jnp.int32, (HALF, HALF), 1)
    low = jnp.where(col > row, codes[:HALF, :HALF], codes[HALF:, HALF:])
    return jnp.concatenate([low, codes[:HALF, HALF:]], axis=1)


def per_device(raw_samples, stack_code, stack_owner):
    x = raw_samples.reshape(2, 704, 128).transpose(1, 0, 2).reshape(1408, 128)
    win = jnp.asarray(np.repeat(window_table(), 2, axis=1))
    wide = call(
        k_channelize, (256, 128), BF16,
        [pltpu.VMEM((1024, 256), BF16), pltpu.VMEM((256, 128), F32)],
        x, win, bf(first_matrix()), jnp.asarray(twiddle_tables()), bf(second_matrix()),
    )
    got = lax.all_to_all(wide.reshape(8, 32, 128), "chan", 0, 0, tiled=True)
    regrouped = call(k_regroup, (256, 128), BF16, [], got.reshape(256, 128))
    spectra = lax.all_to_all(regrouped.reshape(16, 16, 128), "feed", 0, 0, tiled=True)
    codes = fold_codes(lax.all_gather(stack_code, "feed", axis=0, tiled=True))
    owner = jnp.pad(stack_owner, (0, 2), constant_values=-1).reshape(1, NB * 128)
    msgs = call(
        k_stack, (16, 16, 128), F32,
        [
            pltpu.VMEM((2, 256, 128), F32),
            pltpu.VMEM((CHUNK * 32, 128), BF16),
            pltpu.VMEM((CHUNK * 32, 128), BF16),
            pltpu.VMEM((NB * 32 + 16, CHUNK * 256), BF16),
            pltpu.VMEM((128, CHUNK * 256), BF16),
            pltpu.VMEM((NB * 32 + 16, 128), F32),
        ],
        spectra.reshape(256, 128), codes, owner,
    )
    back = lax.all_to_all(msgs, "feed", 0, 0, tiled=True)
    return call(k_finish, (CAP, 2, 256), F32, [], back.reshape(256, 128))


def solution(mesh):
    placed = (P(("feed", "chan"), None), P("feed", None), P())
    return jax.shard_map(
        per_device, mesh=mesh, in_specs=placed, out_specs=P("feed", None, "chan"), check_vma=False
    )
```

```python
import math

import numpy as np
import jax
import jax.numpy as jnp
from jax import lax
from jax.experimental import pallas as pl
from jax.experimental.pallas import tpu as pltpu
from jax.sharding import PartitionSpec as P

SPECTRA = 4
TAPS = 8
FA = 64
FB = 128
FRAME = 8192
STACKS = 382
CAP = 47
FEEDS = 16
GROUPS = 8
INPUTS = 256
HALF = 128
CHUNK = 8
NB = 3
F32 = jnp.float32
BF16 = jnp.bfloat16
NT = (((1,), (1,)), ((), ()))


def window_table():
    length = TAPS * FRAME
    sample = np.arange(length, dtype=np.float64)
    centred = (sample - length / 2 + 0.5) / FRAME
    weights = np.sinc(centred) * (0.5 - 0.5 * np.cos(2.0 * np.pi * (sample + 0.5) / length))
    weights = weights * np.sqrt(FRAME / np.sum(weights * weights))
    return weights.reshape(TAPS, FA, FB).astype(np.float32)


def turns(left, right, modulus):
    return 2.0 * np.pi * (np.outer(left, right) % modulus) / modulus


def first_matrix():
    angles = turns(np.arange(FA), np.arange(FA), FA)
    parts = np.stack([np.cos(angles), -np.sin(angles)]).reshape(2, FA, 4, 16)
    out = np.zeros((2, 4, 2, 16, FA, 2), np.float32)
    for i in range(2):
        out[:, :, i, :, :, i] = parts.transpose(0, 2, 3, 1)
    return out.reshape(256, 128)


def twiddle_tables():
    angles = turns(np.arange(FA), np.arange(FB), FRAME).reshape(4, 1, 16, FB)
    angles = np.broadcast_to(angles, (4, 2, 16, FB)).reshape(128, FB)
    return np.stack([np.cos(angles), np.sin(angles)]).astype(np.float32)


def second_matrix():
    angles = turns(np.arange(32), np.arange(FB), FB)
    return np.concatenate([np.cos(angles), np.sin(angles)], axis=1).astype(np.float32)


def bf(table):
    return jnp.asarray(table).astype(BF16)


def channelize(x_ref, win_ref, first_ref, tw_ref, second_ref, mixed_ref, wide_ref):
    frames = []
    for t in range(SPECTRA):
        total = jnp.zeros((128, FB), F32)
        for p in range(TAPS):
            rows = x_ref[pl.ds((t + p) * 128, 128), :].astype(F32)
            total = total + win_ref[p] * rows
        frames.append(total.astype(BF16))
    frames = jnp.concatenate(frames, axis=1)
    section = jnp.dot(first_ref[...], frames, preferred_element_type=F32)
    cosine, sine = tw_ref[0], tw_ref[1]
    for t in range(SPECTRA):
        re = section[:128, t * FB : (t + 1) * FB]
        im = section[128:, t * FB : (t + 1) * FB]
        real = re * cosine + im * sine
        imag = im * cosine - re * sine
        minus = (-real).astype(BF16)
        real = real.astype(BF16)
        imag = imag.astype(BF16)
        for u in range(8):
            rows = slice(u * 16, u * 16 + 16)
            base = (u * 8 + t) * 16
            mixed_ref[base : base + 16, :FB] = real[rows]
            mixed_ref[base : base + 16, FB:] = imag[rows]
            base = (u * 8 + 4 + t) * 16
            mixed_ref[base : base + 16, :FB] = imag[rows]
            mixed_ref[base : base + 16, FB:] = minus[rows]
    out = lax.dot_general(second_ref[...], mixed_ref[...], NT, preferred_element_type=F32)
    out = out * (1.0 / math.sqrt(FRAME))
    for u in range(8):
        wide_ref[pl.ds(u, 32, stride=8), :] = out[:, u * 128 : (u + 1) * 128]
    return wide_ref[...].astype(BF16)


def regroup(block):
    row = lax.broadcasted_iota(jnp.int32, (256, 256), 0)
    col = lax.broadcasted_iota(jnp.int32, (256, 256), 1)
    source = ((row // 2) % 8) * 32 + (row // 16) * 2 + row % 2
    take = jnp.where(col == source, 1.0, 0.0).astype(BF16)
    return jnp.dot(take, block, preferred_element_type=F32).astype(BF16)


def prepare(code_ref, owner_ref, hi_ref, sign_ref, lo_ref, hot_ref, perm_ref, count_ref):
    codes = code_ref[...].reshape(INPUTS, INPUTS)
    row = lax.broadcasted_iota(jnp.int32, (HALF, HALF), 0)
    col = lax.broadcasted_iota(jnp.int32, (HALF, HALF), 1)
    low = jnp.where(col > row, codes[:HALF, :HALF], codes[HALF:, HALF:])
    code = jnp.concatenate([low, codes[:HALF, HALF:]], axis=1)
    row = lax.broadcasted_iota(jnp.int32, (HALF, INPUTS), 0)
    col = lax.broadcasted_iota(jnp.int32, (HALF, INPUTS), 1)
    target = jnp.where(code >= 0, code, -1 - code)
    sign_ref[...] = jnp.where(code >= 0, 1.0, -1.0).astype(F32)
    hi_ref[...] = lax.shift_right_logical(target, 7)
    lo_ref[...] = jnp.where(col != row, target & 127, -1)
    hot_row = lax.broadcasted_iota(jnp.int32, (128, INPUTS), 0)
    bid = lax.broadcasted_iota(jnp.int32, (16, INPUTS), 0)
    count_ref[...] = jnp.zeros_like(count_ref)

    @pl.loop(0, HALF // CHUNK)
    def _(step):
        marks = []
        hots = []
        for n in range(CHUNK):
            lo = lo_ref[pl.ds(step * CHUNK + n, 1), :]
            hi = hi_ref[pl.ds(step * CHUNK + n, 1), :]
            hots.append(jnp.where(hot_row == lo, 1.0, 0.0).astype(BF16))
            marks.append(jnp.where(hi == bid, 1.0, 0.0).astype(BF16))
        hot = jnp.concatenate(hots, axis=1)
        hot_ref[step] = hot
        mark = jnp.concatenate(marks, axis=1)
        count_ref[...] += lax.dot_general(mark, hot, NT, preferred_element_type=F32)

    owner = owner_ref[...]
    tall = jnp.transpose(jnp.broadcast_to(owner, (128, NB * 128)).astype(F32))
    cols = []
    for b in range(NB):
        mine = owner[:, b * 128 : (b + 1) * 128].astype(F32)
        row = lax.broadcasted_iota(jnp.int32, (NB * 128, 128), 0)
        col = lax.broadcasted_iota(jnp.int32, (NB * 128, 128), 1) + b * 128
        same = jnp.where((tall == mine) & (row < col), 1.0, 0.0)
        cols.append(jnp.sum(same, axis=0, keepdims=True))
    rank = jnp.concatenate(cols, axis=1).astype(jnp.int32)
    place = jnp.where(owner >= 0, owner * 128 + rank, -1)
    later = jnp.where(owner >= 0, place + 64, -1)
    both = jnp.concatenate([place, later], axis=1)
    slot = lax.broadcasted_iota(jnp.int32, (128, 2 * NB * 128), 0)
    for o in range(FEEDS):
        perm_ref[o] = jnp.where(slot + o * 128 == both, 1.0, 0.0).astype(BF16)


def stack_pairs(x_ref, hi_ref, sign_ref, hot_ref, xf_ref, left_ref, right_ref, data_ref, acc_ref):
    x = x_ref[...].reshape(INPUTS, 128)
    xf = x.astype(F32)
    xf_ref[0] = xf
    xf_ref[1] = jnp.concatenate([xf[:, 64:], -xf[:, :64]], axis=1)
    acc_ref[...] = jnp.zeros_like(acc_ref)
    lane = lax.broadcasted_iota(jnp.int32, (16, 128), 1)
    sub = lax.broadcasted_iota(jnp.int32, (16, 128), 0)
    pick = lane % 16 == sub
    lane_j = lax.broadcasted_iota(jnp.int32, (32, 128), 1)

    @pl.loop(0, HALF // CHUNK)
    def _(step):
        base = step * CHUNK
        for n in range(CHUNK):
            for q in range(2):
                at = slice(n * 32 + q * 16, n * 32 + q * 16 + 16)
                row = xf_ref[q, pl.ds(base + n, 1), :]
                left_ref[at, :] = jnp.where(pick, row, 0.0).astype(BF16)
                row = xf_ref[q, pl.ds(HALF + base + n, 1), :]
                right_ref[at, :] = jnp.where(pick, row, 0.0).astype(BF16)
        x = x_ref[...].reshape(INPUTS, 128)
        one = lax.dot_general(left_ref[...], x, NT, preferred_element_type=F32)
        two = lax.dot_general(right_ref[...], x[HALF:], NT, preferred_element_type=F32)
        for n in range(CHUNK):
            at = slice(n * 32, n * 32 + 32)
            low = jnp.where(lane_j > base + n, one[at, :128], two[at, :])
            both = jnp.concatenate([low, one[at, 128:]], axis=1)
            hi = hi_ref[pl.ds(base + n, 1), :]
            sign = sign_ref[pl.ds(base + n, 1), :]
            real = both[:16].astype(BF16)
            imag = (both[16:] * sign).astype(BF16)
            lanes = slice(n * INPUTS, (n + 1) * INPUTS)
            zero = jnp.zeros((), BF16)
            for b in range(NB):
                data_ref[b * 32 : b * 32 + 16, lanes] = jnp.where(hi == b, real, zero)
                data_ref[b * 32 + 16 : b * 32 + 32, lanes] = jnp.where(hi == b, imag, zero)
        acc_ref[...] += lax.dot_general(data_ref[...], hot_ref[step], NT, preferred_element_type=F32)


def messages(acc_ref, count_ref, perm_ref, send_ref):
    parts = []
    for q in range(2):
        for b in range(NB):
            sums = acc_ref[b * 32 + q * 16 : b * 32 + q * 16 + 16, :]
            parts.append(sums / jnp.maximum(count_ref[b : b + 1, :], 1.0))
    means = jnp.concatenate(parts, axis=1)
    high = means.astype(BF16)
    low = (means - high.astype(F32)).astype(BF16)
    both = jnp.concatenate([high, low], axis=0)
    perm = perm_ref[...].reshape(FEEDS * 128, 2 * NB * 128)
    out = lax.dot_general(both, perm, NT, preferred_element_type=F32)
    out = out[:16] + out[16:]
    for o in range(FEEDS):
        send_ref[o] = out[:, o * 128 : (o + 1) * 128]


def finish(block, out_ref):
    turned = jnp.transpose(block)
    out_ref[:, 0, :] = turned[:CAP]
    out_ref[:, 1, :] = turned[64 : 64 + CAP]


def exchange(buffer, target, send_sem, recv_sem, axis, size):
    me = lax.axis_index(axis)
    copies = []
    for d in range(1, size):
        peer = lax.rem(me + d, size)
        copies.append(
            pltpu.make_async_remote_copy(
                src_ref=buffer(peer),
                dst_ref=target.at[me],
                send_sem=send_sem.at[d],
                recv_sem=recv_sem.at[d],
                device_id={axis: peer},
                device_id_type=pl.DeviceIdType.MESH,
            )
        )
    for copy in copies:
        copy.start()

    def arrived():
        for d in range(1, size):
            source = lax.rem(me + size - d, size)
            pltpu.make_async_remote_copy(
                src_ref=buffer(source),
                dst_ref=target.at[source],
                send_sem=send_sem.at[d],
                recv_sem=recv_sem.at[d],
                device_id={axis: source},
                device_id_type=pl.DeviceIdType.MESH,
            ).wait_recv()

    def sent():
        for copy in copies:
            copy.wait_send()

    return arrived, sent


def kernel(
    x_hbm, win_hbm, first_hbm, tw_hbm, second_hbm, code_hbm, owner_hbm, out_ref,
    x_ref, win_ref, first_ref, tw_ref, second_ref, owner_ref,
    mixed_ref, wide_ref, wsend, wrecv, bsend, spec_ref, code_ref,
    hi_ref, sign_ref, lo_ref, hot_ref, perm_ref, count_ref,
    xf_ref, left_ref, right_ref, data_ref, acc_ref, msend, mrecv,
    local_sem, wss, wrs, css, crs, bss, brs, mss, mrs,
):
    feed = lax.axis_index("feed")
    chan = lax.axis_index("chan")
    loads = [
        pltpu.make_async_copy(a, b, local_sem.at[n])
        for n, (a, b) in enumerate([
            (x_hbm, x_ref), (win_hbm, win_ref), (first_hbm, first_ref), (tw_hbm, tw_ref),
            (second_hbm, second_ref), (code_hbm, code_ref.at[feed]), (owner_hbm, owner_ref),
        ])
    ]
    for load in loads:
        load.start()
    barrier = pltpu.get_barrier_semaphore()
    for d in range(1, GROUPS):
        pl.semaphore_signal(
            barrier, inc=1, device_id={"chan": lax.rem(chan + d, GROUPS)},
            device_id_type=pl.DeviceIdType.MESH,
        )
    for d in range(1, FEEDS):
        pl.semaphore_signal(
            barrier, inc=1, device_id={"feed": lax.rem(feed + d, FEEDS)},
            device_id_type=pl.DeviceIdType.MESH,
        )
    for load in loads:
        load.wait()
    wide = channelize(x_ref, win_ref, first_ref, tw_ref, second_ref, mixed_ref, wide_ref)
    wsend[...] = wide.reshape(GROUPS, 32, 128)
    pl.semaphore_wait(barrier, GROUPS + FEEDS - 2)
    w_arrived, w_sent = exchange(lambda d: wsend.at[d], wrecv, wss, wrs, "chan", GROUPS)
    c_arrived, c_sent = exchange(lambda d: code_ref.at[feed], code_ref, css, crs, "feed", FEEDS)
    wrecv[chan] = wsend[chan]
    w_arrived()
    bsend[...] = regroup(wrecv[...].reshape(256, 128)).reshape(FEEDS, 16, 128)
    b_arrived, b_sent = exchange(lambda d: bsend.at[d], spec_ref, bss, brs, "feed", FEEDS)
    spec_ref[feed] = bsend[feed]
    c_arrived()
    prepare(code_ref, owner_ref, hi_ref, sign_ref, lo_ref, hot_ref, perm_ref, count_ref)
    b_arrived()
    stack_pairs(spec_ref, hi_ref, sign_ref, hot_ref, xf_ref, left_ref, right_ref, data_ref, acc_ref)
    messages(acc_ref, count_ref, perm_ref, msend)
    m_arrived, m_sent = exchange(lambda d: msend.at[d], mrecv, mss, mrs, "feed", FEEDS)
    mrecv[feed] = msend[feed]
    m_arrived()
    finish(mrecv[...].reshape(256, 128), out_ref)
    w_sent()
    c_sent()
    b_sent()
    m_sent()


def per_device(raw_samples, stack_code, stack_owner):
    x = raw_samples.reshape(2, 704, 128).transpose(1, 0, 2).reshape(1408, 128)
    win = jnp.asarray(np.repeat(window_table(), 2, axis=1))
    owner = jnp.pad(stack_owner, (0, 2), constant_values=-1).reshape(1, NB * 128)
    rows = NB * 32
    dma = pltpu.SemaphoreType.DMA
    return pl.pallas_call(
        kernel,
        out_shape=jax.ShapeDtypeStruct((CAP, 2, 256), F32),
        in_specs=[pl.BlockSpec(memory_space=pl.ANY)] * 7,
        out_specs=pl.BlockSpec(memory_space=pltpu.VMEM),
        scratch_shapes=[
            pltpu.VMEM((1408, 128), BF16),
            pltpu.VMEM((TAPS, 128, 128), F32),
            pltpu.VMEM((256, 128), BF16),
            pltpu.VMEM((2, 128, 128), F32),
            pltpu.VMEM((32, 256), BF16),
            pltpu.VMEM((1, NB * 128), jnp.int32),
            pltpu.VMEM((1024, 256), BF16),
            pltpu.VMEM((256, 128), F32),
            pltpu.VMEM((GROUPS, 32, 128), BF16),
            pltpu.VMEM((GROUPS, 32, 128), BF16),
            pltpu.VMEM((FEEDS, 16, 128), BF16),
            pltpu.VMEM((FEEDS, 16, 128), BF16),
            pltpu.VMEM((FEEDS, 16, INPUTS), jnp.int32),
            pltpu.VMEM((HALF, INPUTS), jnp.int32),
            pltpu.VMEM((HALF, INPUTS), F32),
            pltpu.VMEM((HALF, INPUTS), jnp.int32),
            pltpu.VMEM((HALF // CHUNK, 128, CHUNK * INPUTS), BF16),
            pltpu.VMEM((FEEDS, 128, 2 * NB * 128), BF16),
            pltpu.VMEM((16, 128), F32),
            pltpu.VMEM((2, INPUTS, 128), F32),
            pltpu.VMEM((CHUNK * 32, 128), BF16),
            pltpu.VMEM((CHUNK * 32, 128), BF16),
            pltpu.VMEM((rows, CHUNK * INPUTS), BF16),
            pltpu.VMEM((rows, 128), F32),
            pltpu.VMEM((FEEDS, 16, 128), F32),
            pltpu.VMEM((FEEDS, 16, 128), F32),
            dma((7,)),
            dma((GROUPS,)), dma((GROUPS,)),
            dma((FEEDS,)), dma((FEEDS,)),
            dma((FEEDS,)), dma((FEEDS,)),
            dma((FEEDS,)), dma((FEEDS,)),
        ],
        compiler_params=pltpu.CompilerParams(
            vmem_limit_bytes=60 << 20, collective_id=0, has_side_effects=True
        ),
    )(x, win, bf(first_matrix()), jnp.asarray(twiddle_tables()), bf(second_matrix()), stack_code, owner)


def solution(mesh):
    placed = (P(("feed", "chan"), None), P("feed", None), P())
    return jax.shard_map(
        per_device, mesh=mesh, in_specs=placed, out_specs=P("feed", None, "chan"), check_vma=False
    )
```

```python
import math

import numpy as np
import jax
import jax.numpy as jnp
from jax import lax
from jax.experimental import pallas as pl
from jax.experimental.pallas import tpu as pltpu
from jax.sharding import PartitionSpec as P

SPECTRA = 4
TAPS = 8
FA = 64
FB = 128
FRAME = 8192
STACKS = 382
CAP = 47
FEEDS = 16
GROUPS = 8
INPUTS = 256
HALF = 128
CHUNK = 8
NB = 3
F32 = jnp.float32
BF16 = jnp.bfloat16
NT = (((1,), (1,)), ((), ()))


def window_table():
    length = TAPS * FRAME
    sample = np.arange(length, dtype=np.float64)
    centred = (sample - length / 2 + 0.5) / FRAME
    weights = np.sinc(centred) * (0.5 - 0.5 * np.cos(2.0 * np.pi * (sample + 0.5) / length))
    weights = weights * np.sqrt(FRAME / np.sum(weights * weights))
    return weights.reshape(TAPS, FA, FB).astype(np.float32)


def turns(left, right, modulus):
    return 2.0 * np.pi * (np.outer(left, right) % modulus) / modulus


def first_matrix():
    angles = turns(np.arange(FA), np.arange(FA), FA)
    parts = np.stack([np.cos(angles), -np.sin(angles)]).reshape(2, FA, 4, 16)
    out = np.zeros((2, 4, 2, 16, FA, 2), np.float32)
    for i in range(2):
        out[:, :, i, :, :, i] = parts.transpose(0, 2, 3, 1)
    return out.reshape(256, 128)


def twiddle_tables():
    angles = turns(np.arange(FA), np.arange(FB), FRAME).reshape(4, 1, 16, FB)
    angles = np.broadcast_to(angles, (4, 2, 16, FB)).reshape(128, FB)
    return np.stack([np.cos(angles), np.sin(angles)]).astype(np.float32)


def second_matrix():
    angles = turns(np.arange(32), np.arange(FB), FB)
    return np.concatenate([np.cos(angles), np.sin(angles)], axis=1).astype(np.float32)


def bf(table):
    return jnp.asarray(table).astype(BF16)


def channelize(x_ref, win_ref, first_ref, tw_ref, second_ref, mixed_ref, wide_ref):
    frames = []
    for t in range(SPECTRA):
        total = jnp.zeros((128, FB), F32)
        for p in range(TAPS):
            rows = x_ref[pl.ds((t + p) * 128, 128), :].astype(F32)
            total = total + win_ref[p] * rows
        frames.append(total.astype(BF16))
    frames = jnp.concatenate(frames, axis=1)
    section = jnp.dot(first_ref[...], frames, preferred_element_type=F32)
    cosine, sine = tw_ref[0], tw_ref[1]
    for t in range(SPECTRA):
        re = section[:128, t * FB : (t + 1) * FB]
        im = section[128:, t * FB : (t + 1) * FB]
        real = re * cosine + im * sine
        imag = im * cosine - re * sine
        minus = (-real).astype(BF16)
        real = real.astype(BF16)
        imag = imag.astype(BF16)
        for u in range(8):
            rows = slice(u * 16, u * 16 + 16)
            base = (u * 8 + t) * 16
            mixed_ref[base : base + 16, :FB] = real[rows]
            mixed_ref[base : base + 16, FB:] = imag[rows]
            base = (u * 8 + 4 + t) * 16
            mixed_ref[base : base + 16, :FB] = imag[rows]
            mixed_ref[base : base + 16, FB:] = minus[rows]
    out = lax.dot_general(second_ref[...], mixed_ref[...], NT, preferred_element_type=F32)
    out = out * (1.0 / math.sqrt(FRAME))
    for u in range(8):
        wide_ref[pl.ds(u, 32, stride=8), :] = out[:, u * 128 : (u + 1) * 128]
    return wide_ref[...].astype(BF16)


def regroup(block):
    row = lax.broadcasted_iota(jnp.int32, (256, 256), 0)
    col = lax.broadcasted_iota(jnp.int32, (256, 256), 1)
    source = ((row // 2) % 8) * 32 + (row // 16) * 2 + row % 2
    take = jnp.where(col == source, 1.0, 0.0).astype(BF16)
    return jnp.dot(take, block, preferred_element_type=F32).astype(BF16)


def permutation(owner_ref, perm_ref):
    owner = owner_ref[...]
    tall = jnp.transpose(jnp.broadcast_to(owner, (128, NB * 128)).astype(F32))
    cols = []
    for b in range(NB):
        mine = owner[:, b * 128 : (b + 1) * 128].astype(F32)
        row = lax.broadcasted_iota(jnp.int32, (NB * 128, 128), 0)
        col = lax.broadcasted_iota(jnp.int32, (NB * 128, 128), 1) + b * 128
        same = jnp.where((tall == mine) & (row < col), 1.0, 0.0)
        cols.append(jnp.sum(same, axis=0, keepdims=True))
    rank = jnp.concatenate(cols, axis=1).astype(jnp.int32)
    place = jnp.where(owner >= 0, owner * 64 + rank, -1)

    @pl.loop(0, FEEDS)
    def _(o):
        slot = lax.broadcasted_iota(jnp.int32, (64, NB * 128), 0) + o * 64
        perm_ref[o] = jnp.where(slot == place, 1.0, 0.0).astype(BF16)


def packed_row(ref, at):
    return jnp.broadcast_to(ref[pl.ds(at, 1), :], (16, ref.shape[1])).astype(BF16)


def prepare(code_ref, hi_ref, sign_ref, lo_ref, hot_ref, count_ref):
    codes = code_ref[...].reshape(INPUTS, INPUTS).astype(jnp.int32)
    row = lax.broadcasted_iota(jnp.int32, (HALF, HALF), 0)
    col = lax.broadcasted_iota(jnp.int32, (HALF, HALF), 1)
    low = jnp.where(col > row, codes[:HALF, :HALF], codes[HALF:, HALF:])
    code = jnp.concatenate([low, codes[:HALF, HALF:]], axis=1)
    row = lax.broadcasted_iota(jnp.int32, (HALF, INPUTS), 0)
    col = lax.broadcasted_iota(jnp.int32, (HALF, INPUTS), 1)
    target = jnp.where(code >= 0, code, -1 - code)
    sign_ref[...] = jnp.where(code >= 0, 1.0, -1.0).astype(F32)
    hi_ref[...] = lax.shift_right_logical(target, 7).astype(F32)
    lo_ref[...] = jnp.where(col != row, target & 127, -1).astype(F32)
    sub = lax.broadcasted_iota(jnp.int32, (16, INPUTS), 0)
    rows = [(sub + r * 16).astype(F32).astype(BF16) for r in range(8)]
    one, zero = jnp.ones((), BF16), jnp.zeros((), BF16)
    count_ref[...] = jnp.zeros_like(count_ref)

    @pl.loop(0, HALF // CHUNK)
    def _(step):
        marks = []
        hots = []
        for n in range(CHUNK):
            lo = packed_row(lo_ref, step * CHUNK + n)
            hi = packed_row(hi_ref, step * CHUNK + n)
            hots.append(jnp.concatenate([jnp.where(lo == rows[r], one, zero) for r in range(8)], axis=0))
            marks.append(jnp.where(hi == rows[0], one, zero))
        hot = jnp.concatenate(hots, axis=1)
        hot_ref[step] = hot
        mark = jnp.concatenate(marks, axis=1)
        count_ref[...] += lax.dot_general(mark, hot, NT, preferred_element_type=F32)


def stack_pairs(x_ref, hi_ref, sign_ref, hot_ref, xf_ref, data_a, data_b, acc_ref):
    x = x_ref[...].reshape(INPUTS, 128)
    xf = x.astype(F32)
    xf_ref[0] = xf
    xf_ref[1] = jnp.concatenate([xf[:, 64:], -xf[:, :64]], axis=1)
    acc_ref[...] = jnp.zeros_like(acc_ref)
    lane = lax.broadcasted_iota(jnp.int32, (16, 128), 1)
    sub = lax.broadcasted_iota(jnp.int32, (16, 128), 0)
    pick = jnp.where(lane % 16 == sub, 1.0, 0.0).astype(BF16)
    lane_j = lax.broadcasted_iota(jnp.int32, (32, 128), 1)
    zero = jnp.zeros((), BF16)

    def produce(step, data_ref):
        base = step * CHUNK
        left, right = [], []
        for n in range(CHUNK):
            for q in range(2):
                left.append(packed_row(xf_ref.at[q], base + n) * pick)
                right.append(packed_row(xf_ref.at[q], HALF + base + n) * pick)
        left = jnp.concatenate(left, axis=0)
        right = jnp.concatenate(right, axis=0)
        x = x_ref[...].reshape(INPUTS, 128)
        one = lax.dot_general(left, x, NT, preferred_element_type=F32)
        two = lax.dot_general(right, x[HALF:], NT, preferred_element_type=F32)
        for n in range(CHUNK):
            at = slice(n * 32, n * 32 + 32)
            low = jnp.where(lane_j > base + n, one[at, :128], two[at, :])
            both = jnp.concatenate([low, one[at, 128:]], axis=1).astype(BF16)
            hi = packed_row(hi_ref, base + n)
            sign = packed_row(sign_ref, base + n)
            real = both[:16]
            imag = both[16:] * sign
            lanes = slice(n * INPUTS, (n + 1) * INPUTS)
            for b in range(NB):
                mine = hi == jnp.full((16, INPUTS), b, BF16)
                data_ref[b * 32 : b * 32 + 16, lanes] = jnp.where(mine, real, zero)
                data_ref[b * 32 + 16 : b * 32 + 32, lanes] = jnp.where(mine, imag, zero)

    def consume(step, data_ref):
        acc_ref[...] += lax.dot_general(data_ref[...], hot_ref[step], NT, preferred_element_type=F32)

    steps = HALF // CHUNK
    produce(0, data_a)

    @pl.loop(0, steps // 2)
    def _(k):
        produce(2 * k + 1, data_b)
        consume(2 * k, data_a)
        produce(jnp.minimum(2 * k + 2, steps - 1), data_a)
        consume(2 * k + 1, data_b)


def messages(acc_ref, count_ref, perm_ref, send_ref):
    parts = []
    for b in range(NB):
        parts.append(acc_ref[b * 32 : b * 32 + 32, :] / jnp.maximum(count_ref[b : b + 1, :], 1.0))
    means = jnp.concatenate(parts, axis=1).astype(BF16)
    perm = perm_ref[...].reshape(FEEDS * 64, NB * 128)
    out = lax.dot_general(means, perm, NT, preferred_element_type=F32)
    first = lax.broadcasted_iota(jnp.int32, (16, 128), 1) < 64
    for o in range(0, FEEDS, 2):
        real = out[:16, o * 64 : o * 64 + 128]
        imag = out[16:, o * 64 : o * 64 + 128]
        send_ref[o] = jnp.where(first, real, pltpu.roll(imag, 64, 1)).astype(BF16)
        send_ref[o + 1] = jnp.where(first, pltpu.roll(real, 64, 1), imag).astype(BF16)


def finish(block, out_ref):
    out_ref[...] = jnp.transpose(block.astype(F32))


def exchange(buffer, target, send_sem, recv_sem, axis, size):
    me = lax.axis_index(axis)
    copies = []
    for d in range(1, size):
        peer = lax.rem(me + d, size)
        copies.append(
            pltpu.make_async_remote_copy(
                src_ref=buffer(peer),
                dst_ref=target.at[me],
                send_sem=send_sem.at[d],
                recv_sem=recv_sem.at[d],
                device_id={axis: peer},
                device_id_type=pl.DeviceIdType.MESH,
            )
        )
    for copy in copies:
        copy.start()

    def arrived():
        for d in range(1, size):
            source = lax.rem(me + size - d, size)
            pltpu.make_async_remote_copy(
                src_ref=buffer(source),
                dst_ref=target.at[source],
                send_sem=send_sem.at[d],
                recv_sem=recv_sem.at[d],
                device_id={axis: source},
                device_id_type=pl.DeviceIdType.MESH,
            ).wait_recv()

    def sent():
        for copy in copies:
            copy.wait_send()

    return arrived, sent


def kernel(
    x_hbm, win_hbm, first_hbm, tw_hbm, second_hbm, code_hbm, owner_hbm, out_ref,
    x_ref, win_ref, first_ref, tw_ref, second_ref, owner_ref, raw_code,
    mixed_ref, wide_ref, wsend, wrecv, bsend, spec_ref, code_ref,
    hi_ref, sign_ref, lo_ref, hot_ref, perm_ref, count_ref,
    xf_ref, data_a, data_b, acc_ref, msend, mrecv,
    local_sem, wss, wrs, css, crs, bss, brs, mss, mrs,
):
    feed = lax.axis_index("feed")
    chan = lax.axis_index("chan")
    loads = [
        pltpu.make_async_copy(a, b, local_sem.at[n])
        for n, (a, b) in enumerate([
            (x_hbm, x_ref), (win_hbm, win_ref), (first_hbm, first_ref), (tw_hbm, tw_ref),
            (second_hbm, second_ref), (code_hbm, raw_code), (owner_hbm, owner_ref),
        ])
    ]
    for load in loads:
        load.start()
    barrier = pltpu.get_barrier_semaphore()
    for d in range(1, GROUPS):
        pl.semaphore_signal(
            barrier, inc=1, device_id={"chan": lax.rem(chan + d, GROUPS)},
            device_id_type=pl.DeviceIdType.MESH,
        )
    for d in range(1, FEEDS):
        pl.semaphore_signal(
            barrier, inc=1, device_id={"feed": lax.rem(feed + d, FEEDS)},
            device_id_type=pl.DeviceIdType.MESH,
        )
    for load in loads:
        load.wait()
    wide = channelize(x_ref, win_ref, first_ref, tw_ref, second_ref, mixed_ref, wide_ref)
    wsend[...] = wide.reshape(GROUPS, 32, 128)
    code_ref[feed] = raw_code[...].astype(jnp.int16)
    permutation(owner_ref, perm_ref)
    pl.semaphore_wait(barrier, GROUPS + FEEDS - 2)
    w_arrived, w_sent = exchange(lambda d: wsend.at[d], wrecv, wss, wrs, "chan", GROUPS)
    c_arrived, c_sent = exchange(lambda d: code_ref.at[feed], code_ref, css, crs, "feed", FEEDS)
    wrecv[chan] = wsend[chan]
    w_arrived()
    bsend[...] = regroup(wrecv[...].reshape(256, 128)).reshape(FEEDS, 16, 128)
    b_arrived, b_sent = exchange(lambda d: bsend.at[d], spec_ref, bss, brs, "feed", FEEDS)
    spec_ref[feed] = bsend[feed]
    c_arrived()
    prepare(code_ref, hi_ref, sign_ref, lo_ref, hot_ref, count_ref)
    b_arrived()
    stack_pairs(spec_ref, hi_ref, sign_ref, hot_ref, xf_ref, data_a, data_b, acc_ref)
    messages(acc_ref, count_ref, perm_ref, msend)
    m_arrived, m_sent = exchange(lambda d: msend.at[d], mrecv, mss, mrs, "feed", FEEDS)
    mrecv[feed] = msend[feed]
    m_arrived()
    finish(mrecv[...].reshape(256, 128), out_ref)
    w_sent()
    c_sent()
    b_sent()
    m_sent()


def per_device(raw_samples, stack_code, stack_owner):
    x = raw_samples.reshape(2, 704, 128).transpose(1, 0, 2).reshape(1408, 128)
    win = jnp.asarray(np.repeat(window_table(), 2, axis=1))
    owner = jnp.pad(stack_owner, (0, 2), constant_values=-1).reshape(1, NB * 128)
    rows = NB * 32
    dma = pltpu.SemaphoreType.DMA
    turned = pl.pallas_call(
        kernel,
        out_shape=jax.ShapeDtypeStruct((128, 256), F32),
        in_specs=[pl.BlockSpec(memory_space=pl.ANY)] * 7,
        out_specs=pl.BlockSpec(memory_space=pltpu.VMEM),
        scratch_shapes=[
            pltpu.VMEM((1408, 128), BF16),
            pltpu.VMEM((TAPS, 128, 128), F32),
            pltpu.VMEM((256, 128), BF16),
            pltpu.VMEM((2, 128, 128), F32),
            pltpu.VMEM((32, 256), BF16),
            pltpu.VMEM((1, NB * 128), jnp.int32),
            pltpu.VMEM((16, INPUTS), jnp.int32),
            pltpu.VMEM((1024, 256), BF16),
            pltpu.VMEM((256, 128), F32),
            pltpu.VMEM((GROUPS, 32, 128), BF16),
            pltpu.VMEM((GROUPS, 32, 128), BF16),
            pltpu.VMEM((FEEDS, 16, 128), BF16),
            pltpu.VMEM((FEEDS, 16, 128), BF16),
            pltpu.VMEM((FEEDS, 16, INPUTS), jnp.int16),
            pltpu.VMEM((HALF, INPUTS), F32),
            pltpu.VMEM((HALF, INPUTS), F32),
            pltpu.VMEM((HALF, INPUTS), F32),
            pltpu.VMEM((HALF // CHUNK, 128, CHUNK * INPUTS), BF16),
            pltpu.VMEM((FEEDS, 64, NB * 128), BF16),
            pltpu.VMEM((16, 128), F32),
            pltpu.VMEM((2, INPUTS, 128), F32),
            pltpu.VMEM((rows, CHUNK * INPUTS), BF16),
            pltpu.VMEM((rows, CHUNK * INPUTS), BF16),
            pltpu.VMEM((rows, 128), F32),
            pltpu.VMEM((FEEDS, 16, 128), BF16),
            pltpu.VMEM((FEEDS, 16, 128), BF16),
            dma((7,)),
            dma((GROUPS,)), dma((GROUPS,)),
            dma((FEEDS,)), dma((FEEDS,)),
            dma((FEEDS,)), dma((FEEDS,)),
            dma((FEEDS,)), dma((FEEDS,)),
        ],
        compiler_params=pltpu.CompilerParams(
            vmem_limit_bytes=60 << 20, collective_id=0, has_side_effects=True
        ),
    )(x, win, bf(first_matrix()), jnp.asarray(twiddle_tables()), bf(second_matrix()), stack_code, owner)
    return turned.reshape(2, 64, 256)[:, :CAP].transpose(1, 0, 2)


def solution(mesh):
    placed = (P(("feed", "chan"), None), P("feed", None), P())
    return jax.shard_map(
        per_device, mesh=mesh, in_specs=placed, out_specs=P("feed", None, "chan"), check_vma=False
    )
```

```python
import math

import numpy as np
import jax
import jax.numpy as jnp
from jax import lax
from jax.experimental import pallas as pl
from jax.experimental.pallas import tpu as pltpu
from jax.sharding import PartitionSpec as P

SPECTRA = 4
TAPS = 8
FA = 64
FB = 128
FRAME = 8192
STACKS = 382
CAP = 47
FEEDS = 16
GROUPS = 8
INPUTS = 256
HALF = 128
CHUNK = 8
NB = 3
F32 = jnp.float32
BF16 = jnp.bfloat16
NT = (((1,), (1,)), ((), ()))


def window_table():
    length = TAPS * FRAME
    sample = np.arange(length, dtype=np.float64)
    centred = (sample - length / 2 + 0.5) / FRAME
    weights = np.sinc(centred) * (0.5 - 0.5 * np.cos(2.0 * np.pi * (sample + 0.5) / length))
    weights = weights * np.sqrt(FRAME / np.sum(weights * weights))
    return weights.reshape(TAPS, FA, FB).astype(np.float32)


def turns(left, right, modulus):
    return 2.0 * np.pi * (np.outer(left, right) % modulus) / modulus


def first_matrix():
    angles = turns(np.arange(FA), np.arange(FA), FA)
    parts = np.stack([np.cos(angles), -np.sin(angles)]).reshape(2, FA, 4, 16)
    out = np.zeros((2, 4, 2, 16, FA, 2), np.float32)
    for i in range(2):
        out[:, :, i, :, :, i] = parts.transpose(0, 2, 3, 1)
    return out.reshape(256, 128)


def twiddle_tables():
    angles = turns(np.arange(FA), np.arange(FB), FRAME).reshape(4, 1, 16, FB)
    angles = np.broadcast_to(angles, (4, 2, 16, FB)).reshape(128, FB)
    return np.stack([np.cos(angles), np.sin(angles)]).astype(np.float32)


def second_matrix():
    angles = turns(np.arange(32), np.arange(FB), FB)
    return np.concatenate([np.cos(angles), np.sin(angles)], axis=1).astype(np.float32)


def bf(table):
    return jnp.asarray(table).astype(BF16)


def channelize(x_ref, win_ref, first_ref, tw_ref, second_ref, mixed_ref, wide_ref):
    frames = []
    for t in range(SPECTRA):
        total = jnp.zeros((128, FB), F32)
        for p in range(TAPS):
            rows = x_ref[pl.ds((t + p) * 128, 128), :].astype(F32)
            total = total + win_ref[p] * rows
        frames.append(total.astype(BF16))
    frames = jnp.concatenate(frames, axis=1)
    section = jnp.dot(first_ref[...], frames, preferred_element_type=F32)
    cosine, sine = tw_ref[0], tw_ref[1]
    for t in range(SPECTRA):
        re = section[:128, t * FB : (t + 1) * FB]
        im = section[128:, t * FB : (t + 1) * FB]
        real = re * cosine + im * sine
        imag = im * cosine - re * sine
        minus = (-real).astype(BF16)
        real = real.astype(BF16)
        imag = imag.astype(BF16)
        for u in range(8):
            rows = slice(u * 16, u * 16 + 16)
            base = (u * 8 + t) * 16
            mixed_ref[base : base + 16, :FB] = real[rows]
            mixed_ref[base : base + 16, FB:] = imag[rows]
            base = (u * 8 + 4 + t) * 16
            mixed_ref[base : base + 16, :FB] = imag[rows]
            mixed_ref[base : base + 16, FB:] = minus[rows]
    out = lax.dot_general(second_ref[...], mixed_ref[...], NT, preferred_element_type=F32)
    out = out * (1.0 / math.sqrt(FRAME))
    for u in range(8):
        wide_ref[pl.ds(u, 32, stride=8), :] = out[:, u * 128 : (u + 1) * 128]
    return wide_ref[...].astype(BF16)


def regroup(block):
    row = lax.broadcasted_iota(jnp.int32, (256, 256), 0)
    col = lax.broadcasted_iota(jnp.int32, (256, 256), 1)
    source = ((row // 2) % 8) * 32 + (row // 16) * 2 + row % 2
    take = jnp.where(col == source, 1.0, 0.0).astype(BF16)
    return jnp.dot(take, block, preferred_element_type=F32).astype(BF16)


def permutation(owner_ref, perm_ref):
    owner = jnp.concatenate([owner_ref[...].reshape(1, STACKS), jnp.full((1, NB * 128 - STACKS), -1, jnp.int32)], axis=1)
    tall = jnp.transpose(jnp.broadcast_to(owner, (128, NB * 128)).astype(F32))
    cols = []
    for b in range(NB):
        mine = owner[:, b * 128 : (b + 1) * 128].astype(F32)
        row = lax.broadcasted_iota(jnp.int32, (NB * 128, 128), 0)
        col = lax.broadcasted_iota(jnp.int32, (NB * 128, 128), 1) + b * 128
        same = jnp.where((tall == mine) & (row < col), 1.0, 0.0)
        cols.append(jnp.sum(same, axis=0, keepdims=True))
    rank = jnp.concatenate(cols, axis=1).astype(jnp.int32)
    place = jnp.where(owner >= 0, owner * 64 + rank, -1)

    @pl.loop(0, FEEDS)
    def _(o):
        slot = lax.broadcasted_iota(jnp.int32, (64, NB * 128), 0) + o * 64
        perm_ref[o] = jnp.where(slot == place, 1.0, 0.0).astype(BF16)


def packed_row(ref, at):
    return jnp.broadcast_to(ref[pl.ds(at, 1), :], (16, ref.shape[1])).astype(BF16)


def prepare(code_ref, hi_ref, sign_ref, lo_ref, hot_ref, count_ref):
    codes = code_ref[...].reshape(INPUTS, INPUTS).astype(jnp.int32)
    row = lax.broadcasted_iota(jnp.int32, (HALF, HALF), 0)
    col = lax.broadcasted_iota(jnp.int32, (HALF, HALF), 1)
    low = jnp.where(col > row, codes[:HALF, :HALF], codes[HALF:, HALF:])
    code = jnp.concatenate([low, codes[:HALF, HALF:]], axis=1)
    row = lax.broadcasted_iota(jnp.int32, (HALF, INPUTS), 0)
    col = lax.broadcasted_iota(jnp.int32, (HALF, INPUTS), 1)
    target = jnp.where(code >= 0, code, -1 - code)
    sign_ref[...] = jnp.where(code >= 0, 1.0, -1.0).astype(F32)
    hi_ref[...] = lax.shift_right_logical(target, 7).astype(F32)
    lo_ref[...] = jnp.where(col != row, target & 127, -1).astype(F32)
    sub = lax.broadcasted_iota(jnp.int32, (16, INPUTS), 0)
    rows = [(sub + r * 16).astype(F32).astype(BF16) for r in range(8)]
    one, zero = jnp.ones((), BF16), jnp.zeros((), BF16)
    count_ref[...] = jnp.zeros_like(count_ref)

    @pl.loop(0, HALF // CHUNK)
    def _(step):
        marks = []
        hots = []
        for n in range(CHUNK):
            lo = packed_row(lo_ref, step * CHUNK + n)
            hi = packed_row(hi_ref, step * CHUNK + n)
            hot = jnp.concatenate([jnp.where(lo == rows[r], one, zero) for r in range(8)], axis=0)
            hot_ref[step, 2 * n] = hot[:, :128]
            hot_ref[step, 2 * n + 1] = hot[:, 128:]
            hots.append(hot)
            marks.append(jnp.where(hi == rows[0], one, zero))
        hot = jnp.concatenate(hots, axis=1)
        mark = jnp.concatenate(marks, axis=1)
        count_ref[...] += lax.dot_general(mark, hot, NT, preferred_element_type=F32)


def stack_pairs(x_ref, hi_ref, sign_ref, hot_ref, xf_ref, data_a, data_b, acc_ref):
    x = x_ref[...].reshape(INPUTS, 128)
    xf = x.astype(F32)
    xf_ref[0] = xf
    xf_ref[1] = jnp.concatenate([xf[:, 64:], -xf[:, :64]], axis=1)
    acc_ref[...] = jnp.zeros_like(acc_ref)
    lane = lax.broadcasted_iota(jnp.int32, (16, 128), 1)
    sub = lax.broadcasted_iota(jnp.int32, (16, 128), 0)
    pick = jnp.where(lane % 16 == sub, 1.0, 0.0).astype(BF16)
    lane_j = lax.broadcasted_iota(jnp.int32, (32, 128), 1)
    zero = jnp.zeros((), BF16)

    def produce(step, data_ref):
        base = step * CHUNK
        left, right = [], []
        for n in range(CHUNK):
            for q in range(2):
                left.append(packed_row(xf_ref.at[q], base + n) * pick)
                right.append(packed_row(xf_ref.at[q], HALF + base + n) * pick)
        left = jnp.concatenate(left, axis=0)
        right = jnp.concatenate(right, axis=0)
        x = x_ref[...].reshape(INPUTS, 128)
        one = lax.dot_general(left, x, NT, preferred_element_type=F32)
        two = lax.dot_general(right, x[HALF:], NT, preferred_element_type=F32)
        for n in range(CHUNK):
            at = slice(n * 32, n * 32 + 32)
            low = jnp.where(lane_j > base + n, one[at, :128], two[at, :])
            both = jnp.concatenate([low, one[at, 128:]], axis=1).astype(BF16)
            hi = packed_row(hi_ref, base + n)
            sign = packed_row(sign_ref, base + n)
            real = both[:16]
            imag = both[16:] * sign
            for b in range(NB):
                mine = hi == jnp.full((16, INPUTS), b, BF16)
                re = jnp.where(mine, real, zero)
                im = jnp.where(mine, imag, zero)
                for h in range(2):
                    half = slice(h * 128, h * 128 + 128)
                    data_ref[2 * n + h, b * 32 : b * 32 + 16, :] = re[:, half]
                    data_ref[2 * n + h, b * 32 + 16 : b * 32 + 32, :] = im[:, half]

    def consume(step, data_ref):
        data = jnp.concatenate([data_ref[m] for m in range(2 * CHUNK)], axis=1)
        hot = jnp.concatenate([hot_ref[step, m] for m in range(2 * CHUNK)], axis=1)
        acc_ref[...] += lax.dot_general(data, hot, NT, preferred_element_type=F32)

    steps = HALF // CHUNK
    produce(0, data_a)

    @pl.loop(0, steps // 2)
    def _(k):
        produce(2 * k + 1, data_b)
        consume(2 * k, data_a)
        produce(jnp.minimum(2 * k + 2, steps - 1), data_a)
        consume(2 * k + 1, data_b)


def messages(acc_ref, count_ref, perm_ref, send_ref):
    parts = []
    for b in range(NB):
        parts.append(acc_ref[b * 32 : b * 32 + 32, :] / jnp.maximum(count_ref[b : b + 1, :], 1.0))
    means = jnp.concatenate(parts, axis=1).astype(BF16)
    perm = perm_ref[...].reshape(FEEDS * 64, NB * 128)
    out = lax.dot_general(means, perm, NT, preferred_element_type=F32)
    first = lax.broadcasted_iota(jnp.int32, (16, 128), 1) < 64
    for o in range(0, FEEDS, 2):
        real = out[:16, o * 64 : o * 64 + 128]
        imag = out[16:, o * 64 : o * 64 + 128]
        send_ref[o] = jnp.where(first, real, pltpu.roll(imag, 64, 1)).astype(BF16)
        send_ref[o + 1] = jnp.where(first, pltpu.roll(real, 64, 1), imag).astype(BF16)


def finish(block, out_ref):
    turned = jnp.transpose(block.astype(F32))
    for h in range(2):
        for q in range(2):
            out_ref[pl.ds(2 * h + q, CAP, stride=4), :] = turned[q * 64 : q * 64 + CAP, h * 128 : h * 128 + 128]


def far_first(axis):
    if axis == "feed":
        sizes, weights = (4, 2, 2), ((0, 3, 6, 3), (0, 6), (0, 1))
    else:
        sizes, weights = (4, 2), ((0, 3, 6, 3), (0, 3))
    offsets = [o for o in np.ndindex(*sizes) if any(o)]
    offsets.sort(key=lambda o: -sum(w[n] for w, n in zip(weights, o)))
    return sizes, offsets


def peers(axis):
    me = lax.axis_index(axis)
    sizes, offsets = far_first(axis)
    place, rest = [], me
    for size in reversed(sizes):
        place.insert(0, lax.rem(rest, size))
        rest = rest // size
    out = []
    for offset in offsets:
        peer = 0
        for size, at, step in zip(sizes, place, offset):
            peer = peer * size + lax.rem(at + step, size)
        out.append(peer)
    return out


def exchange(buffer, target, send_sem, recv_sem, axis):
    me = lax.axis_index(axis)
    others = peers(axis)
    for peer in others:
        pltpu.make_async_remote_copy(
            src_ref=buffer(peer),
            dst_ref=target.at[me],
            send_sem=send_sem,
            recv_sem=recv_sem,
            device_id={axis: peer},
            device_id_type=pl.DeviceIdType.MESH,
        ).start()
    whole = target.at[pl.ds(0, len(others))]
    every = pltpu.make_async_remote_copy(
        src_ref=whole,
        dst_ref=whole,
        send_sem=send_sem,
        recv_sem=recv_sem,
        device_id={axis: others[0]},
        device_id_type=pl.DeviceIdType.MESH,
    )
    return every.wait_recv, every.wait_send


def kernel(
    x_hbm, win_hbm, first_hbm, tw_hbm, second_hbm, code_hbm, owner_hbm, out_ref,
    x_ref, win_ref, first_ref, tw_ref, second_ref, owner_ref, raw_code,
    mixed_ref, wide_ref, wsend, wrecv, bsend, spec_ref, code_ref,
    hi_ref, sign_ref, lo_ref, hot_ref, perm_ref, count_ref,
    xf_ref, data_a, data_b, acc_ref, msend, mrecv,
    local_sem, wss, wrs, css, crs, bss, brs, mss, mrs,
):
    feed = lax.axis_index("feed")
    chan = lax.axis_index("chan")
    barrier = pltpu.get_barrier_semaphore()
    for axis in ("chan", "feed"):
        for peer in peers(axis):
            pl.semaphore_signal(
                barrier, inc=1, device_id={axis: peer}, device_id_type=pl.DeviceIdType.MESH
            )
    loads = [
        pltpu.make_async_copy(a, b, local_sem.at[n])
        for n, (a, b) in enumerate([
            (x_hbm, x_ref), (win_hbm, win_ref), (first_hbm, first_ref), (tw_hbm, tw_ref),
            (second_hbm, second_ref), (code_hbm, raw_code), (owner_hbm, owner_ref),
        ])
    ]
    for load in loads:
        load.start()
    for load in loads:
        load.wait()
    wide = channelize(x_ref, win_ref, first_ref, tw_ref, second_ref, mixed_ref, wide_ref)
    wsend[...] = wide.reshape(GROUPS, 32, 128)
    code_ref[feed] = raw_code[...].astype(jnp.int16)
    permutation(owner_ref, perm_ref)
    pl.semaphore_wait(barrier, GROUPS + FEEDS - 2)
    w_arrived, w_sent = exchange(lambda d: wsend.at[d], wrecv, wss, wrs, "chan")
    c_arrived, c_sent = exchange(lambda d: code_ref.at[feed], code_ref, css, crs, "feed")
    wrecv[chan] = wsend[chan]
    w_arrived()
    bsend[...] = regroup(wrecv[...].reshape(256, 128)).reshape(FEEDS, 16, 128)
    b_arrived, b_sent = exchange(lambda d: bsend.at[d], spec_ref, bss, brs, "feed")
    spec_ref[feed] = bsend[feed]
    c_arrived()
    prepare(code_ref, hi_ref, sign_ref, lo_ref, hot_ref, count_ref)
    b_arrived()
    stack_pairs(spec_ref, hi_ref, sign_ref, hot_ref, xf_ref, data_a, data_b, acc_ref)
    messages(acc_ref, count_ref, perm_ref, msend)
    m_arrived, m_sent = exchange(lambda d: msend.at[d], mrecv, mss, mrs, "feed")
    mrecv[feed] = msend[feed]
    m_arrived()
    finish(mrecv[...].reshape(256, 128), out_ref)
    w_sent()
    c_sent()
    b_sent()
    m_sent()


def per_device(raw_samples, stack_code, stack_owner):
    x = raw_samples.reshape(2, 704, 128).transpose(1, 0, 2).reshape(1408, 128)
    win = jnp.asarray(np.repeat(window_table(), 2, axis=1))
    owner = stack_owner
    rows = NB * 32
    dma = pltpu.SemaphoreType.DMA
    turned = pl.pallas_call(
        kernel,
        out_shape=jax.ShapeDtypeStruct((4 * CAP, 128), F32),
        in_specs=[pl.BlockSpec(memory_space=pl.ANY)] * 7,
        out_specs=pl.BlockSpec(memory_space=pltpu.VMEM),
        scratch_shapes=[
            pltpu.VMEM((1408, 128), BF16),
            pltpu.VMEM((TAPS, 128, 128), F32),
            pltpu.VMEM((256, 128), BF16),
            pltpu.VMEM((2, 128, 128), F32),
            pltpu.VMEM((32, 256), BF16),
            pltpu.VMEM((STACKS,), jnp.int32),
            pltpu.VMEM((16, INPUTS), jnp.int32),
            pltpu.VMEM((1024, 256), BF16),
            pltpu.VMEM((256, 128), F32),
            pltpu.VMEM((GROUPS, 32, 128), BF16),
            pltpu.VMEM((GROUPS, 32, 128), BF16),
            pltpu.VMEM((FEEDS, 16, 128), BF16),
            pltpu.VMEM((FEEDS, 16, 128), BF16),
            pltpu.VMEM((FEEDS, 16, INPUTS), jnp.int16),
            pltpu.VMEM((HALF, INPUTS), F32),
            pltpu.VMEM((HALF, INPUTS), F32),
            pltpu.VMEM((HALF, INPUTS), F32),
            pltpu.VMEM((HALF // CHUNK, 2 * CHUNK, 128, 128), BF16),
            pltpu.VMEM((FEEDS, 64, NB * 128), BF16),
            pltpu.VMEM((16, 128), F32),
            pltpu.VMEM((2, INPUTS, 128), F32),
            pltpu.VMEM((2 * CHUNK, rows, 128), BF16),
            pltpu.VMEM((2 * CHUNK, rows, 128), BF16),
            pltpu.VMEM((rows, 128), F32),
            pltpu.VMEM((FEEDS, 16, 128), BF16),
            pltpu.VMEM((FEEDS, 16, 128), BF16),
            dma((7,)),
            dma, dma, dma, dma, dma, dma, dma, dma,
        ],
        compiler_params=pltpu.CompilerParams(
            vmem_limit_bytes=60 << 20, collective_id=0, has_side_effects=True
        ),
    )(x, win, bf(first_matrix()), jnp.asarray(twiddle_tables()), bf(second_matrix()), stack_code, owner)
    return turned.reshape(CAP, 2, 2, 128).transpose(0, 2, 1, 3).reshape(CAP, 2, 256)


def solution(mesh):
    placed = (P(("feed", "chan"), None), P("feed", None), P())
    return jax.shard_map(
        per_device, mesh=mesh, in_specs=placed, out_specs=P("feed", None, "chan"), check_vma=False
    )
```

```python
import math

import numpy as np
import jax
import jax.numpy as jnp
from jax import lax
from jax.experimental import pallas as pl
from jax.experimental.pallas import tpu as pltpu
from jax.sharding import PartitionSpec as P

SPECTRA = 4
TAPS = 8
FA = 64
FB = 128
FRAME = 8192
STACKS = 382
CAP = 47
FEEDS = 16
GROUPS = 8
INPUTS = 256
HALF = 128
CHUNK = 8
UNROLL = 4
AHEAD = 0
NB = 3
F32 = jnp.float32
BF16 = jnp.bfloat16
NT = (((1,), (1,)), ((), ()))


def window_table():
    length = TAPS * FRAME
    sample = np.arange(length, dtype=np.float64)
    centred = (sample - length / 2 + 0.5) / FRAME
    weights = np.sinc(centred) * (0.5 - 0.5 * np.cos(2.0 * np.pi * (sample + 0.5) / length))
    weights = weights * np.sqrt(FRAME / np.sum(weights * weights))
    return weights.reshape(TAPS, FA, FB).astype(np.float32)


def turns(left, right, modulus):
    return 2.0 * np.pi * (np.outer(left, right) % modulus) / modulus


def first_matrix():
    angles = turns(np.arange(FA), np.arange(FA), FA)
    parts = np.stack([np.cos(angles), -np.sin(angles)]).reshape(2, FA, 4, 16)
    out = np.zeros((2, 4, 2, 16, FA, 2), np.float32)
    for i in range(2):
        out[:, :, i, :, :, i] = parts.transpose(0, 2, 3, 1)
    return out.reshape(256, 128)


def twiddle_tables():
    angles = turns(np.arange(FA), np.arange(FB), FRAME).reshape(4, 1, 16, FB)
    angles = np.broadcast_to(angles, (4, 2, 16, FB)).reshape(128, FB)
    return np.stack([np.cos(angles), np.sin(angles)]).astype(np.float32)


def second_matrix():
    angles = turns(np.arange(32), np.arange(FB), FB)
    return np.concatenate([np.cos(angles), np.sin(angles)], axis=1).astype(np.float32)


def bf(table):
    return jnp.asarray(table).astype(BF16)


def channelize(x_ref, win_ref, first_ref, tw_ref, second_ref, mixed_ref, wide_ref):
    frames = []
    for t in range(SPECTRA):
        total = jnp.zeros((128, FB), F32)
        for p in range(TAPS):
            rows = x_ref[pl.ds((t + p) * 128, 128), :].astype(F32)
            total = total + win_ref[p] * rows
        frames.append(total.astype(BF16))
    frames = jnp.concatenate(frames, axis=1)
    section = jnp.dot(first_ref[...], frames, preferred_element_type=F32)
    cosine, sine = tw_ref[0], tw_ref[1]
    for t in range(SPECTRA):
        re = section[:128, t * FB : (t + 1) * FB]
        im = section[128:, t * FB : (t + 1) * FB]
        real = re * cosine + im * sine
        imag = im * cosine - re * sine
        minus = (-real).astype(BF16)
        real = real.astype(BF16)
        imag = imag.astype(BF16)
        for u in range(8):
            rows = slice(u * 16, u * 16 + 16)
            base = (u * 8 + t) * 16
            mixed_ref[base : base + 16, :FB] = real[rows]
            mixed_ref[base : base + 16, FB:] = imag[rows]
            base = (u * 8 + 4 + t) * 16
            mixed_ref[base : base + 16, :FB] = imag[rows]
            mixed_ref[base : base + 16, FB:] = minus[rows]
    out = lax.dot_general(second_ref[...], mixed_ref[...], NT, preferred_element_type=F32)
    out = out * (1.0 / math.sqrt(FRAME))
    for u in range(8):
        wide_ref[pl.ds(u, 32, stride=8), :] = out[:, u * 128 : (u + 1) * 128]
    return wide_ref[...].astype(BF16)


def regroup(block):
    row = lax.broadcasted_iota(jnp.int32, (256, 256), 0)
    col = lax.broadcasted_iota(jnp.int32, (256, 256), 1)
    source = ((row // 2) % 8) * 32 + (row // 16) * 2 + row % 2
    take = jnp.where(col == source, 1.0, 0.0).astype(BF16)
    return jnp.dot(take, block, preferred_element_type=F32).astype(BF16)


def permutation(owner_ref, perm_ref):
    owner = jnp.concatenate([owner_ref[...].reshape(1, STACKS), jnp.full((1, NB * 128 - STACKS), -1, jnp.int32)], axis=1)
    tall = jnp.transpose(jnp.broadcast_to(owner, (128, NB * 128)).astype(F32))
    cols = []
    for b in range(NB):
        mine = owner[:, b * 128 : (b + 1) * 128].astype(F32)
        row = lax.broadcasted_iota(jnp.int32, (NB * 128, 128), 0)
        col = lax.broadcasted_iota(jnp.int32, (NB * 128, 128), 1) + b * 128
        same = jnp.where((tall == mine) & (row < col), 1.0, 0.0)
        cols.append(jnp.sum(same, axis=0, keepdims=True))
    rank = jnp.concatenate(cols, axis=1).astype(jnp.int32)
    place = jnp.where(owner >= 0, owner * 64 + rank, -1)

    @pl.loop(0, FEEDS)
    def _(o):
        slot = lax.broadcasted_iota(jnp.int32, (64, NB * 128), 0) + o * 64
        perm_ref[o] = jnp.where(slot == place, 1.0, 0.0).astype(BF16)


def packed_row(ref, at):
    return jnp.broadcast_to(ref[pl.ds(at, 1), :], (16, ref.shape[1])).astype(BF16)


def unpack_codes(code_ref, hi_ref, sign_ref, lo_ref):
    codes = code_ref[...].reshape(INPUTS, INPUTS).astype(jnp.int32)
    row = lax.broadcasted_iota(jnp.int32, (HALF, HALF), 0)
    col = lax.broadcasted_iota(jnp.int32, (HALF, HALF), 1)
    low = jnp.where(col > row, codes[:HALF, :HALF], codes[HALF:, HALF:])
    code = jnp.concatenate([low, codes[:HALF, HALF:]], axis=1)
    row = lax.broadcasted_iota(jnp.int32, (HALF, INPUTS), 0)
    col = lax.broadcasted_iota(jnp.int32, (HALF, INPUTS), 1)
    target = jnp.where(code >= 0, code, -1 - code)
    sign_ref[...] = jnp.where(code >= 0, 1.0, -1.0).astype(F32)
    hi_ref[...] = lax.shift_right_logical(target, 7).astype(F32)
    lo_ref[...] = jnp.where(col != row, target & 127, -1).astype(F32)


def row_ids():
    sub = lax.broadcasted_iota(jnp.int32, (16, INPUTS), 0)
    return [(sub + r * 16).astype(F32).astype(BF16) for r in range(8)]


def one_hot(lo_ref, at, rows):
    one, zero = jnp.ones((), BF16), jnp.zeros((), BF16)
    lo = packed_row(lo_ref, at)
    return jnp.concatenate([jnp.where(lo == rows[r], one, zero) for r in range(8)], axis=0)


def prepare(lo_ref, hot_ref):
    rows = row_ids()

    @pl.loop(0, AHEAD * UNROLL)
    def _(step):
        for n in range(CHUNK):
            hot = one_hot(lo_ref, step * CHUNK + n, rows)
            hot_ref[step, 256 * n : 256 * n + 128, :] = hot[:, :128]
            hot_ref[step, 256 * n + 128 : 256 * n + 256, :] = hot[:, 128:]


def count_pairs(hi_ref, lo_ref, count_ref):
    rows = row_ids()
    one, zero = jnp.ones((), BF16), jnp.zeros((), BF16)
    count_ref[...] = jnp.zeros_like(count_ref)

    @pl.loop(0, HALF // CHUNK)
    def _(step):
        hots = [one_hot(lo_ref, step * CHUNK + n, rows) for n in range(CHUNK)]
        marks = [jnp.where(packed_row(hi_ref, step * CHUNK + n) == rows[0], one, zero) for n in range(CHUNK)]
        hot = jnp.concatenate(hots, axis=1)
        mark = jnp.concatenate(marks, axis=1)
        count_ref[...] += lax.dot_general(mark, hot, NT, preferred_element_type=F32)


def stack_pairs(x_ref, hi_ref, sign_ref, lo_ref, hot_ref, xf_ref, acc_ref):
    x = x_ref[...].reshape(INPUTS, 128)
    xf = x.astype(F32)
    xf_ref[0] = xf
    xf_ref[1] = jnp.concatenate([xf[:, 64:], -xf[:, :64]], axis=1)
    acc_ref[...] = jnp.zeros_like(acc_ref)
    lane = lax.broadcasted_iota(jnp.int32, (16, 128), 1)
    sub = lax.broadcasted_iota(jnp.int32, (16, 128), 0)
    pick = jnp.where(lane % 16 == sub, 1.0, 0.0).astype(BF16)
    lane_j = lax.broadcasted_iota(jnp.int32, (32, 128), 1)
    zero = jnp.zeros((), BF16)

    ids = row_ids()

    def produce(step, ready):
        base = step * CHUNK
        left, right = [], []
        for n in range(CHUNK):
            for q in range(2):
                left.append(packed_row(xf_ref.at[q], base + n) * pick)
                right.append(packed_row(xf_ref.at[q], HALF + base + n) * pick)
        left = jnp.concatenate(left, axis=0)
        right = jnp.concatenate(right, axis=0)
        x = x_ref[...].reshape(INPUTS, 128)
        one = lax.dot_general(left, x, NT, preferred_element_type=F32)
        two = lax.dot_general(right, x[HALF:], NT, preferred_element_type=F32)
        data = []
        for n in range(CHUNK):
            at = slice(n * 32, n * 32 + 32)
            low = jnp.where(lane_j > base + n, one[at, :128], two[at, :])
            both = jnp.concatenate([low, one[at, 128:]], axis=1).astype(BF16)
            hi = packed_row(hi_ref, base + n)
            sign = packed_row(sign_ref, base + n)
            parts = []
            for b in range(NB):
                mine = hi == jnp.full((16, INPUTS), b, BF16)
                parts.append(jnp.where(mine, both[:16], zero))
                parts.append(jnp.where(mine, both[16:] * sign, zero))
            data.append(jnp.concatenate(parts, axis=0))
        if ready:
            hot = [hot_ref[step, m * 128 : m * 128 + 128] for m in range(2 * CHUNK)]
        else:
            hot = [one_hot(lo_ref, base + n, ids) for n in range(CHUNK)]
        return data, hot

    def product(data, hot):
        data = jnp.concatenate(data, axis=1)
        hot = jnp.concatenate(hot, axis=1)
        return lax.dot_general(data, hot, NT, preferred_element_type=F32)

    def sweep(first, last, ready):
        @pl.loop(first, last)
        def _(k):
            data, hot = [], []
            for u in range(UNROLL):
                d, h = produce(k * UNROLL + u, ready)
                data += d
                hot += h
            acc_ref[...] += product(data, hot)

    if AHEAD:
        sweep(0, AHEAD, True)
    if AHEAD < HALF // CHUNK // UNROLL:
        sweep(AHEAD, HALF // CHUNK // UNROLL, False)


def messages(acc_ref, perm_ref, send_ref):
    sums = jnp.concatenate([acc_ref[b * 32 : b * 32 + 32, :] for b in range(NB)], axis=1).astype(BF16)
    perm = perm_ref[...].reshape(FEEDS * 64, NB * 128)
    out = lax.dot_general(sums, perm, NT, preferred_element_type=F32)
    first = lax.broadcasted_iota(jnp.int32, (16, 128), 1) < 64
    for o in range(0, FEEDS, 2):
        real = out[:16, o * 64 : o * 64 + 128]
        imag = out[16:, o * 64 : o * 64 + 128]
        send_ref[o] = jnp.where(first, real, pltpu.roll(imag, 64, 1)).astype(BF16)
        send_ref[o + 1] = jnp.where(first, pltpu.roll(real, 64, 1), imag).astype(BF16)


def slot_scale(count_ref, perm):
    count = jnp.concatenate([count_ref[b : b + 1, :] for b in range(NB)], axis=1)
    high = jnp.floor(count * (1.0 / 256.0))
    digit = lax.broadcasted_iota(jnp.int32, (16, NB * 128), 0)
    digits = jnp.where(digit == 0, high, count - 256.0 * high).astype(BF16)
    got = lax.dot_general(perm, digits, NT, preferred_element_type=F32)
    return 1.0 / jnp.maximum(256.0 * got[:, 0:1] + got[:, 1:2], 1.0)


def finish(block, scale, out_ref):
    turned = jnp.transpose(block.astype(F32))
    for h in range(2):
        for q in range(2):
            mean = turned[q * 64 : q * 64 + CAP, h * 128 : h * 128 + 128] * scale[:CAP]
            out_ref[pl.ds(2 * h + q, CAP, stride=4), :] = mean


def far_first(axis):
    if axis == "feed":
        sizes, weights = (4, 2, 2), ((0, 3, 6, 3), (0, 6), (0, 1))
    else:
        sizes, weights = (4, 2), ((0, 3, 6, 3), (0, 3))
    offsets = [o for o in np.ndindex(*sizes) if any(o)]
    offsets.sort(key=lambda o: -sum(w[n] for w, n in zip(weights, o)))
    return sizes, offsets


def peers(axis):
    me = lax.axis_index(axis)
    sizes, offsets = far_first(axis)
    place, rest = [], me
    for size in reversed(sizes):
        place.insert(0, lax.rem(rest, size))
        rest = rest // size
    out = []
    for offset in offsets:
        peer = 0
        for size, at, step in zip(sizes, place, offset):
            peer = peer * size + lax.rem(at + step, size)
        out.append(peer)
    return out


def exchange(buffer, target, send_sem, recv_sem, axis):
    me = lax.axis_index(axis)
    others = peers(axis)
    for peer in others:
        pltpu.make_async_remote_copy(
            src_ref=buffer(peer),
            dst_ref=target.at[me],
            send_sem=send_sem,
            recv_sem=recv_sem,
            device_id={axis: peer},
            device_id_type=pl.DeviceIdType.MESH,
        ).start()
    whole = target.at[pl.ds(0, len(others))]
    every = pltpu.make_async_remote_copy(
        src_ref=whole,
        dst_ref=whole,
        send_sem=send_sem,
        recv_sem=recv_sem,
        device_id={axis: others[0]},
        device_id_type=pl.DeviceIdType.MESH,
    )
    return every.wait_recv, every.wait_send


def kernel(
    x_hbm, win_hbm, first_hbm, tw_hbm, second_hbm, code_hbm, owner_hbm, out_ref,
    x_ref, win_ref, first_ref, tw_ref, second_ref, owner_ref, raw_code,
    mixed_ref, wide_ref, wsend, wrecv, bsend, spec_ref, code_ref,
    hi_ref, sign_ref, lo_ref, hot_ref, perm_ref, count_ref,
    xf_ref, acc_ref, msend, mrecv,
    known, local_sem, wss, wrs, css, crs, bss, brs, mss, mrs,
):
    feed = lax.axis_index("feed")
    chan = lax.axis_index("chan")
    z, yc = feed // 4, lax.rem(feed, 4)
    y, c = yc // 2, lax.rem(yc, 2)
    along_z = [{"feed": lax.rem(z + d, 4) * 4 + yc} for d in (2, 1, 3)]
    along_yc = [
        {"feed": z * 4 + lax.rem(y + e, 2) * 2 + lax.rem(c + d, 2)} for e, d in ((1, 1), (1, 0), (0, 1))
    ]
    barrier = pltpu.get_barrier_semaphore()
    for device in [{"chan": peer} for peer in peers("chan")] + along_z + along_yc:
        pl.semaphore_signal(barrier, inc=1, device_id=device, device_id_type=pl.DeviceIdType.MESH)
    loads = [
        pltpu.make_async_copy(a, b, local_sem.at[n])
        for n, (a, b) in enumerate([
            (x_hbm, x_ref), (win_hbm, win_ref), (first_hbm, first_ref), (tw_hbm, tw_ref),
            (second_hbm, second_ref), (code_hbm, raw_code), (owner_hbm, owner_ref),
        ])
    ]
    for load in loads:
        load.start()
    for load in loads:
        load.wait()
    wide = channelize(x_ref, win_ref, first_ref, tw_ref, second_ref, mixed_ref, wide_ref)
    wsend[...] = wide.reshape(GROUPS, 32, 128)
    code_ref[feed] = raw_code[...].astype(jnp.int16)
    permutation(owner_ref, perm_ref)
    pl.semaphore_wait(barrier, 13)
    for device in along_z:
        pl.semaphore_signal(known, inc=1, device_id=device, device_id_type=pl.DeviceIdType.MESH)
    w_arrived, w_sent = exchange(lambda d: wsend.at[d], wrecv, wss, wrs, "chan")
    wrecv[chan] = wsend[chan]
    pl.semaphore_wait(known, 3)
    c_arrived, c_sent = exchange(lambda d: code_ref.at[feed], code_ref, css, crs, "feed")
    w_arrived()
    bsend[...] = regroup(wrecv[...].reshape(256, 128)).reshape(FEEDS, 16, 128)
    b_arrived, b_sent = exchange(lambda d: bsend.at[d], spec_ref, bss, brs, "feed")
    spec_ref[feed] = bsend[feed]
    c_arrived()
    unpack_codes(code_ref, hi_ref, sign_ref, lo_ref)
    prepare(lo_ref, hot_ref)
    b_arrived()
    stack_pairs(spec_ref, hi_ref, sign_ref, lo_ref, hot_ref, xf_ref, acc_ref)
    messages(acc_ref, perm_ref, msend)
    m_arrived, m_sent = exchange(lambda d: msend.at[d], mrecv, mss, mrs, "feed")
    mrecv[feed] = msend[feed]
    count_pairs(hi_ref, lo_ref, count_ref)
    scale = slot_scale(count_ref, perm_ref[feed])
    m_arrived()
    finish(mrecv[...].reshape(256, 128), scale, out_ref)
    w_sent()
    c_sent()
    b_sent()
    m_sent()


def per_device(raw_samples, stack_code, stack_owner):
    x = raw_samples.reshape(2, 704, 128).transpose(1, 0, 2).reshape(1408, 128)
    win = jnp.asarray(np.repeat(window_table(), 2, axis=1))
    owner = stack_owner
    rows = NB * 32
    dma = pltpu.SemaphoreType.DMA
    turned = pl.pallas_call(
        kernel,
        out_shape=jax.ShapeDtypeStruct((4 * CAP, 128), F32),
        in_specs=[pl.BlockSpec(memory_space=pl.ANY)] * 7,
        out_specs=pl.BlockSpec(memory_space=pltpu.VMEM),
        scratch_shapes=[
            pltpu.VMEM((1408, 128), BF16),
            pltpu.VMEM((TAPS, 128, 128), F32),
            pltpu.VMEM((256, 128), BF16),
            pltpu.VMEM((2, 128, 128), F32),
            pltpu.VMEM((32, 256), BF16),
            pltpu.VMEM((STACKS,), jnp.int32),
            pltpu.VMEM((16, INPUTS), jnp.int32),
            pltpu.VMEM((1024, 256), BF16),
            pltpu.VMEM((256, 128), F32),
            pltpu.VMEM((GROUPS, 32, 128), BF16),
            pltpu.VMEM((GROUPS, 32, 128), BF16),
            pltpu.VMEM((FEEDS, 16, 128), BF16),
            pltpu.VMEM((FEEDS, 16, 128), BF16),
            pltpu.VMEM((FEEDS, 16, INPUTS), jnp.int16),
            pltpu.VMEM((HALF, INPUTS), F32),
            pltpu.VMEM((HALF, INPUTS), F32),
            pltpu.VMEM((HALF, INPUTS), F32),
            pltpu.VMEM((HALF // CHUNK, 2 * CHUNK * 128, 128), BF16),
            pltpu.VMEM((FEEDS, 64, NB * 128), BF16),
            pltpu.VMEM((16, 128), F32),
            pltpu.VMEM((2, INPUTS, 128), F32),
            pltpu.VMEM((rows, 128), F32),
            pltpu.VMEM((FEEDS, 16, 128), BF16),
            pltpu.VMEM((FEEDS, 16, 128), BF16),
            pltpu.SemaphoreType.REGULAR,
            dma((7,)),
            dma, dma, dma, dma, dma, dma, dma, dma,
        ],
        compiler_params=pltpu.CompilerParams(
            vmem_limit_bytes=60 << 20, collective_id=0, has_side_effects=True
        ),
    )(x, win, bf(first_matrix()), jnp.asarray(twiddle_tables()), bf(second_matrix()), stack_code, owner)
    return turned.reshape(CAP, 2, 2, 128).transpose(0, 2, 1, 3).reshape(CAP, 2, 256)


def solution(mesh):
    placed = (P(("feed", "chan"), None), P("feed", None), P())
    return jax.shard_map(
        per_device, mesh=mesh, in_specs=placed, out_specs=P("feed", None, "chan"), check_vma=False
    )
```

```python
import math

import numpy as np
import jax
import jax.numpy as jnp
from jax import lax
from jax.experimental import pallas as pl
from jax.experimental.pallas import tpu as pltpu
from jax.sharding import PartitionSpec as P

SPECTRA = 4
TAPS = 8
FA = 64
FB = 128
FRAME = 8192
STACKS = 382
CAP = 47
FEEDS = 16
GROUPS = 8
INPUTS = 256
HALF = 128
CHUNK = 16
UNROLL = 8
EARLY = 4
NB = 3
F32 = jnp.float32
BF16 = jnp.bfloat16
NT = (((1,), (1,)), ((), ()))


def window_table():
    length = TAPS * FRAME
    sample = np.arange(length, dtype=np.float64)
    centred = (sample - length / 2 + 0.5) / FRAME
    weights = np.sinc(centred) * (0.5 - 0.5 * np.cos(2.0 * np.pi * (sample + 0.5) / length))
    weights = weights * np.sqrt(FRAME / np.sum(weights * weights))
    return weights.reshape(TAPS, FA, FB).astype(np.float32)


def turns(left, right, modulus):
    return 2.0 * np.pi * (np.outer(left, right) % modulus) / modulus


def first_matrix():
    angles = turns(np.arange(FA), np.arange(FA), FA)
    parts = np.stack([np.cos(angles), -np.sin(angles)]).reshape(2, FA, 4, 16)
    out = np.zeros((2, 4, 2, 16, FA, 2), np.float32)
    for i in range(2):
        out[:, :, i, :, :, i] = parts.transpose(0, 2, 3, 1)
    return out.reshape(256, 128)


def twiddle_tables():
    angles = turns(np.arange(FA), np.arange(FB), FRAME).reshape(4, 1, 16, FB)
    angles = np.broadcast_to(angles, (4, 2, 16, FB)).reshape(128, FB)
    return np.stack([np.cos(angles), np.sin(angles)]).astype(np.float32)


def second_matrix():
    angles = turns(np.arange(32), np.arange(FB), FB)
    return np.concatenate([np.cos(angles), np.sin(angles)], axis=1).astype(np.float32)


def bf(table):
    return jnp.asarray(table).astype(BF16)


def channelize(x_ref, win_ref, first_ref, tw_ref, second_ref, mixed_ref, wide_ref):
    frames = []
    for t in range(SPECTRA):
        total = jnp.zeros((128, FB), F32)
        for p in range(TAPS):
            rows = x_ref[pl.ds((t + p) * 128, 128), :].astype(F32)
            total = total + win_ref[p] * rows
        frames.append(total.astype(BF16))
    frames = jnp.concatenate(frames, axis=1)
    section = jnp.dot(first_ref[...], frames, preferred_element_type=F32)
    cosine, sine = tw_ref[0], tw_ref[1]
    for t in range(SPECTRA):
        re = section[:128, t * FB : (t + 1) * FB]
        im = section[128:, t * FB : (t + 1) * FB]
        real = re * cosine + im * sine
        imag = im * cosine - re * sine
        minus = (-real).astype(BF16)
        real = real.astype(BF16)
        imag = imag.astype(BF16)
        for u in range(8):
            rows = slice(u * 16, u * 16 + 16)
            base = (u * 8 + t) * 16
            mixed_ref[base : base + 16, :FB] = real[rows]
            mixed_ref[base : base + 16, FB:] = imag[rows]
            base = (u * 8 + 4 + t) * 16
            mixed_ref[base : base + 16, :FB] = imag[rows]
            mixed_ref[base : base + 16, FB:] = minus[rows]
    out = lax.dot_general(second_ref[...], mixed_ref[...], NT, preferred_element_type=F32)
    out = out * (1.0 / math.sqrt(FRAME))
    for u in range(8):
        wide_ref[pl.ds(u, 32, stride=8), :] = out[:, u * 128 : (u + 1) * 128]
    return wide_ref[...].astype(BF16)


def regroup(block):
    row = lax.broadcasted_iota(jnp.int32, (256, 256), 0)
    col = lax.broadcasted_iota(jnp.int32, (256, 256), 1)
    source = ((row // 2) % 8) * 32 + (row // 16) * 2 + row % 2
    take = jnp.where(col == source, 1.0, 0.0).astype(BF16)
    return jnp.dot(take, block, preferred_element_type=F32).astype(BF16)


def permutation(owner_ref, perm_ref):
    owner = jnp.concatenate([owner_ref[...].reshape(1, STACKS), jnp.full((1, NB * 128 - STACKS), -1, jnp.int32)], axis=1)
    tall = jnp.transpose(jnp.broadcast_to(owner, (128, NB * 128)).astype(F32))
    cols = []
    for b in range(NB):
        mine = owner[:, b * 128 : (b + 1) * 128].astype(F32)
        row = lax.broadcasted_iota(jnp.int32, (NB * 128, 128), 0)
        col = lax.broadcasted_iota(jnp.int32, (NB * 128, 128), 1) + b * 128
        same = jnp.where((tall == mine) & (row < col), 1.0, 0.0)
        cols.append(jnp.sum(same, axis=0, keepdims=True))
    rank = jnp.concatenate(cols, axis=1).astype(jnp.int32)
    place = jnp.where(owner >= 0, owner * 64 + rank, -1)

    @pl.loop(0, FEEDS)
    def _(o):
        slot = lax.broadcasted_iota(jnp.int32, (64, NB * 128), 0) + o * 64
        perm_ref[o] = jnp.where(slot == place, 1.0, 0.0).astype(BF16)


def packed_row(ref, at):
    return jnp.broadcast_to(ref[pl.ds(at, 1), :], (16, ref.shape[1])).astype(BF16)


def unpack_codes(code_ref, hi_ref, sign_ref, lo_ref):
    codes = code_ref[...].reshape(INPUTS, INPUTS).astype(jnp.int32)
    row = lax.broadcasted_iota(jnp.int32, (HALF, HALF), 0)
    col = lax.broadcasted_iota(jnp.int32, (HALF, HALF), 1)
    low = jnp.where(col > row, codes[:HALF, :HALF], codes[HALF:, HALF:])
    code = jnp.concatenate([low, codes[:HALF, HALF:]], axis=1)
    row = lax.broadcasted_iota(jnp.int32, (HALF, INPUTS), 0)
    col = lax.broadcasted_iota(jnp.int32, (HALF, INPUTS), 1)
    target = jnp.where(code >= 0, code, -1 - code)
    sign_ref[...] = jnp.where(code >= 0, 1.0, -1.0).astype(F32)
    hi_ref[...] = lax.shift_right_logical(target, 7).astype(F32)
    lo_ref[...] = jnp.where(col != row, target & 127, -1).astype(F32)


def row_ids():
    sub = lax.broadcasted_iota(jnp.int32, (16, INPUTS), 0)
    return [(sub + r * 16).astype(F32).astype(BF16) for r in range(8)]


def one_hot(lo_ref, at, rows):
    one, zero = jnp.ones((), BF16), jnp.zeros((), BF16)
    lo = packed_row(lo_ref, at)
    return jnp.concatenate([jnp.where(lo == rows[r], one, zero) for r in range(8)], axis=0)


def count_pairs(first, last, hi_ref, lo_ref, count_ref):
    rows = row_ids()
    one, zero = jnp.ones((), BF16), jnp.zeros((), BF16)

    @pl.loop(first, last)
    def _(step):
        hots = [one_hot(lo_ref, step * CHUNK + n, rows) for n in range(CHUNK)]
        marks = [jnp.where(packed_row(hi_ref, step * CHUNK + n) == rows[0], one, zero) for n in range(CHUNK)]
        hot = jnp.concatenate(hots, axis=1)
        mark = jnp.concatenate(marks, axis=1)
        count_ref[...] += lax.dot_general(mark, hot, NT, preferred_element_type=F32)


def stack_pairs(x_ref, hi_ref, sign_ref, lo_ref, xf_ref, acc_ref):
    x = x_ref[...].reshape(INPUTS, 128)
    xf = x.astype(F32)
    xf_ref[0] = xf
    xf_ref[1] = jnp.concatenate([xf[:, 64:], -xf[:, :64]], axis=1)
    acc_ref[...] = jnp.zeros_like(acc_ref)
    lane = lax.broadcasted_iota(jnp.int32, (16, 128), 1)
    sub = lax.broadcasted_iota(jnp.int32, (16, 128), 0)
    pick = jnp.where(lane % 16 == sub, 1.0, 0.0).astype(BF16)
    lane_j = lax.broadcasted_iota(jnp.int32, (32, 128), 1)
    zero = jnp.zeros((), BF16)

    ids = row_ids()

    def produce(step):
        base = step * CHUNK
        left, right = [], []
        for n in range(CHUNK):
            for q in range(2):
                left.append(packed_row(xf_ref.at[q], base + n) * pick)
                right.append(packed_row(xf_ref.at[q], HALF + base + n) * pick)
        left = jnp.concatenate(left, axis=0)
        right = jnp.concatenate(right, axis=0)
        x = x_ref[...].reshape(INPUTS, 128)
        one = lax.dot_general(left, x, NT, preferred_element_type=F32)
        two = lax.dot_general(right, x[HALF:], NT, preferred_element_type=F32)
        data = []
        for n in range(CHUNK):
            at = slice(n * 32, n * 32 + 32)
            low = jnp.where(lane_j > base + n, one[at, :128], two[at, :])
            both = jnp.concatenate([low, one[at, 128:]], axis=1).astype(BF16)
            hi = packed_row(hi_ref, base + n)
            sign = packed_row(sign_ref, base + n)
            parts = []
            for b in range(NB):
                mine = hi == jnp.full((16, INPUTS), b, BF16)
                parts.append(jnp.where(mine, both[:16], zero))
                parts.append(jnp.where(mine, both[16:] * sign, zero))
            data.append(jnp.concatenate(parts, axis=0))
        hot = [one_hot(lo_ref, base + n, ids) for n in range(CHUNK)]
        return data, hot

    def product(data, hot):
        data = jnp.concatenate(data, axis=1)
        hot = jnp.concatenate(hot, axis=1)
        return lax.dot_general(hot, data, NT, preferred_element_type=F32)

    @pl.loop(0, HALF // CHUNK // UNROLL)
    def _(k):
        data, hot = [], []
        for u in range(UNROLL):
            d, h = produce(k * UNROLL + u)
            data += d
            hot += h
        acc_ref[...] += product(data, hot)


def messages(acc_ref, perm_ref, send_ref):
    turned = jnp.transpose(jnp.concatenate([acc_ref[...], jnp.zeros((128, 32), F32)], axis=1))
    sums = jnp.concatenate([turned[b * 32 : b * 32 + 32, :] for b in range(NB)], axis=1).astype(BF16)
    perm = perm_ref[...].reshape(FEEDS * 64, NB * 128)
    out = lax.dot_general(sums, perm, NT, preferred_element_type=F32)
    first = lax.broadcasted_iota(jnp.int32, (16, 128), 1) < 64
    for o in range(0, FEEDS, 2):
        real = out[:16, o * 64 : o * 64 + 128]
        imag = out[16:, o * 64 : o * 64 + 128]
        send_ref[o] = jnp.where(first, real, pltpu.roll(imag, 64, 1)).astype(BF16)
        send_ref[o + 1] = jnp.where(first, pltpu.roll(real, 64, 1), imag).astype(BF16)


def slot_scale(count_ref, perm):
    count = jnp.concatenate([count_ref[b : b + 1, :] for b in range(NB)], axis=1)
    high = jnp.floor(count * (1.0 / 256.0))
    digit = lax.broadcasted_iota(jnp.int32, (16, NB * 128), 0)
    digits = jnp.where(digit == 0, high, count - 256.0 * high).astype(BF16)
    got = lax.dot_general(perm, digits, NT, preferred_element_type=F32)
    return 1.0 / jnp.maximum(256.0 * got[:, 0:1] + got[:, 1:2], 1.0)


def finish(block, scale, out_ref):
    turned = jnp.transpose(block.astype(F32))
    for h in range(2):
        for q in range(2):
            mean = turned[q * 64 : q * 64 + CAP, h * 128 : h * 128 + 128] * scale[:CAP]
            out_ref[pl.ds(2 * h + q, CAP, stride=4), :] = mean


def far_first(axis):
    if axis == "feed":
        sizes, weights = (4, 2, 2), ((0, 3, 6, 3), (0, 6), (0, 1))
    else:
        sizes, weights = (4, 2), ((0, 3, 6, 3), (0, 3))
    offsets = [o for o in np.ndindex(*sizes) if any(o)]
    offsets.sort(key=lambda o: -sum(w[n] for w, n in zip(weights, o)))
    return sizes, offsets


def peers(axis):
    me = lax.axis_index(axis)
    sizes, offsets = far_first(axis)
    place, rest = [], me
    for size in reversed(sizes):
        place.insert(0, lax.rem(rest, size))
        rest = rest // size
    out = []
    for offset in offsets:
        peer = 0
        for size, at, step in zip(sizes, place, offset):
            peer = peer * size + lax.rem(at + step, size)
        out.append(peer)
    return out


def exchange(buffer, target, send_sem, recv_sem, axis):
    me = lax.axis_index(axis)
    others = peers(axis)
    for peer in others:
        pltpu.make_async_remote_copy(
            src_ref=buffer(peer),
            dst_ref=target.at[me],
            send_sem=send_sem,
            recv_sem=recv_sem,
            device_id={axis: peer},
            device_id_type=pl.DeviceIdType.MESH,
        ).start()
    whole = target.at[pl.ds(0, len(others))]
    every = pltpu.make_async_remote_copy(
        src_ref=whole,
        dst_ref=whole,
        send_sem=send_sem,
        recv_sem=recv_sem,
        device_id={axis: others[0]},
        device_id_type=pl.DeviceIdType.MESH,
    )
    return every.wait_recv, every.wait_send


def kernel(
    x_hbm, win_hbm, first_hbm, tw_hbm, second_hbm, code_hbm, owner_hbm, out_ref,
    x_ref, win_ref, first_ref, tw_ref, second_ref, owner_ref, raw_code,
    mixed_ref, wide_ref, wsend, wrecv, bsend, spec_ref, code_ref,
    hi_ref, sign_ref, lo_ref, perm_ref, count_ref,
    xf_ref, acc_ref, msend, mrecv,
    known, local_sem, wss, wrs, css, crs, bss, brs, mss, mrs,
):
    feed = lax.axis_index("feed")
    chan = lax.axis_index("chan")
    z, yc = feed // 4, lax.rem(feed, 4)
    y, c = yc // 2, lax.rem(yc, 2)
    along_z = [{"feed": lax.rem(z + d, 4) * 4 + yc} for d in (2, 1, 3)]
    along_yc = [
        {"feed": z * 4 + lax.rem(y + e, 2) * 2 + lax.rem(c + d, 2)} for e, d in ((1, 1), (1, 0), (0, 1))
    ]
    barrier = pltpu.get_barrier_semaphore()
    for device in [{"chan": peer} for peer in peers("chan")] + along_z + along_yc:
        pl.semaphore_signal(barrier, inc=1, device_id=device, device_id_type=pl.DeviceIdType.MESH)
    loads = [
        pltpu.make_async_copy(a, b, local_sem.at[n])
        for n, (a, b) in enumerate([
            (x_hbm, x_ref), (win_hbm, win_ref), (first_hbm, first_ref), (tw_hbm, tw_ref),
            (second_hbm, second_ref), (code_hbm, raw_code), (owner_hbm, owner_ref),
        ])
    ]
    for load in loads:
        load.start()
    for load in loads:
        load.wait()
    wide = channelize(x_ref, win_ref, first_ref, tw_ref, second_ref, mixed_ref, wide_ref)
    wsend[...] = wide.reshape(GROUPS, 32, 128)
    code_ref[feed] = raw_code[...].astype(jnp.int16)
    permutation(owner_ref, perm_ref)
    pl.semaphore_wait(barrier, 13)
    for device in along_z:
        pl.semaphore_signal(known, inc=1, device_id=device, device_id_type=pl.DeviceIdType.MESH)
    w_arrived, w_sent = exchange(lambda d: wsend.at[d], wrecv, wss, wrs, "chan")
    wrecv[chan] = wsend[chan]
    pl.semaphore_wait(known, 3)
    c_arrived, c_sent = exchange(lambda d: code_ref.at[feed], code_ref, css, crs, "feed")
    w_arrived()
    bsend[...] = regroup(wrecv[...].reshape(256, 128)).reshape(FEEDS, 16, 128)
    b_arrived, b_sent = exchange(lambda d: bsend.at[d], spec_ref, bss, brs, "feed")
    spec_ref[feed] = bsend[feed]
    c_arrived()
    unpack_codes(code_ref, hi_ref, sign_ref, lo_ref)
    count_ref[...] = jnp.zeros_like(count_ref)
    count_pairs(0, EARLY, hi_ref, lo_ref, count_ref)
    b_arrived()
    stack_pairs(spec_ref, hi_ref, sign_ref, lo_ref, xf_ref, acc_ref)
    messages(acc_ref, perm_ref, msend)
    m_arrived, m_sent = exchange(lambda d: msend.at[d], mrecv, mss, mrs, "feed")
    mrecv[feed] = msend[feed]
    count_pairs(EARLY, HALF // CHUNK, hi_ref, lo_ref, count_ref)
    scale = slot_scale(count_ref, perm_ref[feed])
    m_arrived()
    finish(mrecv[...].reshape(256, 128), scale, out_ref)
    w_sent()
    c_sent()
    b_sent()
    m_sent()


def per_device(raw_samples, stack_code, stack_owner):
    x = raw_samples.reshape(2, 704, 128).transpose(1, 0, 2).reshape(1408, 128)
    win = jnp.asarray(np.repeat(window_table(), 2, axis=1))
    owner = stack_owner
    rows = NB * 32
    dma = pltpu.SemaphoreType.DMA
    turned = pl.pallas_call(
        kernel,
        out_shape=jax.ShapeDtypeStruct((4 * CAP, 128), F32),
        in_specs=[pl.BlockSpec(memory_space=pl.ANY)] * 7,
        out_specs=pl.BlockSpec(memory_space=pltpu.VMEM),
        scratch_shapes=[
            pltpu.VMEM((1408, 128), BF16),
            pltpu.VMEM((TAPS, 128, 128), F32),
            pltpu.VMEM((256, 128), BF16),
            pltpu.VMEM((2, 128, 128), F32),
            pltpu.VMEM((32, 256), BF16),
            pltpu.VMEM((STACKS,), jnp.int32),
            pltpu.VMEM((16, INPUTS), jnp.int32),
            pltpu.VMEM((1024, 256), BF16),
            pltpu.VMEM((256, 128), F32),
            pltpu.VMEM((GROUPS, 32, 128), BF16),
            pltpu.VMEM((GROUPS, 32, 128), BF16),
            pltpu.VMEM((FEEDS, 16, 128), BF16),
            pltpu.VMEM((FEEDS, 16, 128), BF16),
            pltpu.VMEM((FEEDS, 16, INPUTS), jnp.int16),
            pltpu.VMEM((HALF, INPUTS), F32),
            pltpu.VMEM((HALF, INPUTS), F32),
            pltpu.VMEM((HALF, INPUTS), F32),
            pltpu.VMEM((FEEDS, 64, NB * 128), BF16),
            pltpu.VMEM((16, 128), F32),
            pltpu.VMEM((2, INPUTS, 128), F32),
            pltpu.VMEM((128, rows), F32),
            pltpu.VMEM((FEEDS, 16, 128), BF16),
            pltpu.VMEM((FEEDS, 16, 128), BF16),
            pltpu.SemaphoreType.REGULAR,
            dma((7,)),
            dma, dma, dma, dma, dma, dma, dma, dma,
        ],
        compiler_params=pltpu.CompilerParams(
            vmem_limit_bytes=60 << 20, collective_id=0, has_side_effects=True
        ),
    )(x, win, bf(first_matrix()), jnp.asarray(twiddle_tables()), bf(second_matrix()), stack_code, owner)
    return turned.reshape(CAP, 2, 2, 128).transpose(0, 2, 1, 3).reshape(CAP, 2, 256)


def solution(mesh):
    placed = (P(("feed", "chan"), None), P("feed", None), P())
    return jax.shard_map(
        per_device, mesh=mesh, in_specs=placed, out_specs=P("feed", None, "chan"), check_vma=False
    )
```

```python
import math

import numpy as np
import jax
import jax.numpy as jnp
from jax import lax
from jax.experimental import pallas as pl
from jax.experimental.pallas import tpu as pltpu
from jax.sharding import PartitionSpec as P

SPECTRA = 4
TAPS = 8
FA = 64
FB = 128
FRAME = 8192
STACKS = 382
CAP = 47
FEEDS = 16
GROUPS = 8
INPUTS = 256
HALF = 128
CHUNK = 16
UNROLL = 8
EARLY = 4
NB = 3
F32 = jnp.float32
BF16 = jnp.bfloat16
NT = (((1,), (1,)), ((), ()))


def window_table():
    length = TAPS * FRAME
    sample = np.arange(length, dtype=np.float64)
    centred = (sample - length / 2 + 0.5) / FRAME
    weights = np.sinc(centred) * (0.5 - 0.5 * np.cos(2.0 * np.pi * (sample + 0.5) / length))
    weights = weights * np.sqrt(FRAME / np.sum(weights * weights))
    return weights.reshape(TAPS, FA, FB).astype(np.float32)


def turns(left, right, modulus):
    return 2.0 * np.pi * (np.outer(left, right) % modulus) / modulus


def first_matrix():
    angles = turns(np.arange(FA), np.arange(FA), FA)
    parts = np.stack([np.cos(angles), -np.sin(angles)]).reshape(2, FA, 4, 16)
    out = np.zeros((2, 4, 2, 16, FA, 2), np.float32)
    for i in range(2):
        out[:, :, i, :, :, i] = parts.transpose(0, 2, 3, 1)
    return out.reshape(256, 128)


def twiddle_tables():
    angles = turns(np.arange(FA), np.arange(FB), FRAME).reshape(4, 1, 16, FB)
    angles = np.broadcast_to(angles, (4, 2, 16, FB)).reshape(128, FB)
    return np.stack([np.cos(angles), np.sin(angles)]).astype(np.float32)


def second_matrix():
    angles = turns(np.arange(32), np.arange(FB), FB)
    return np.concatenate([np.cos(angles), np.sin(angles)], axis=1).astype(np.float32)


def bf(table):
    return jnp.asarray(table).astype(BF16)


def channelize(x_ref, win_ref, first_ref, tw_ref, second_ref, mixed_ref, wide_ref):
    frames = []
    for t in range(SPECTRA):
        total = jnp.zeros((128, FB), F32)
        for p in range(TAPS):
            rows = x_ref[pl.ds((t + p) * 128, 128), :].astype(F32)
            total = total + win_ref[p] * rows
        frames.append(total.astype(BF16))
    frames = jnp.concatenate(frames, axis=1)
    section = jnp.dot(first_ref[...], frames, preferred_element_type=F32)
    cosine, sine = tw_ref[0], tw_ref[1]
    for t in range(SPECTRA):
        re = section[:128, t * FB : (t + 1) * FB]
        im = section[128:, t * FB : (t + 1) * FB]
        real = re * cosine + im * sine
        imag = im * cosine - re * sine
        minus = (-real).astype(BF16)
        real = real.astype(BF16)
        imag = imag.astype(BF16)
        for u in range(8):
            rows = slice(u * 16, u * 16 + 16)
            base = (u * 8 + t) * 16
            mixed_ref[base : base + 16, :FB] = real[rows]
            mixed_ref[base : base + 16, FB:] = imag[rows]
            base = (u * 8 + 4 + t) * 16
            mixed_ref[base : base + 16, :FB] = imag[rows]
            mixed_ref[base : base + 16, FB:] = minus[rows]
    out = lax.dot_general(second_ref[...], mixed_ref[...], NT, preferred_element_type=F32)
    out = out * (1.0 / math.sqrt(FRAME))
    for u in range(8):
        wide_ref[pl.ds(u, 32, stride=8), :] = out[:, u * 128 : (u + 1) * 128]
    return wide_ref[...].astype(BF16)


def regroup_matrix():
    row = lax.broadcasted_iota(jnp.int32, (256, 256), 0)
    col = lax.broadcasted_iota(jnp.int32, (256, 256), 1)
    source = ((row // 2) % 8) * 32 + (row // 16) * 2 + row % 2
    return jnp.where(col == source, 1.0, 0.0).astype(BF16)


def permutation(owner_ref, perm_ref):
    owner = jnp.concatenate([owner_ref[...].reshape(1, STACKS), jnp.full((1, NB * 128 - STACKS), -1, jnp.int32)], axis=1)
    tall = jnp.transpose(jnp.broadcast_to(owner, (128, NB * 128)).astype(F32))
    cols = []
    for b in range(NB):
        mine = owner[:, b * 128 : (b + 1) * 128].astype(F32)
        row = lax.broadcasted_iota(jnp.int32, (NB * 128, 128), 0)
        col = lax.broadcasted_iota(jnp.int32, (NB * 128, 128), 1) + b * 128
        same = jnp.where((tall == mine) & (row < col), 1.0, 0.0)
        cols.append(jnp.sum(same, axis=0, keepdims=True))
    rank = jnp.concatenate(cols, axis=1).astype(jnp.int32)
    place = jnp.where(owner >= 0, owner * 64 + rank, -1)

    @pl.loop(0, FEEDS)
    def _(o):
        slot = lax.broadcasted_iota(jnp.int32, (64, NB * 128), 0) + o * 64
        perm_ref[o] = jnp.where(slot == place, 1.0, 0.0).astype(BF16)


def packed_row(ref, at):
    return jnp.broadcast_to(ref[pl.ds(at, 1), :], (16, ref.shape[1])).astype(BF16)


def unpack_codes(code_ref, hi_ref, sign_ref, lo_ref):
    codes = code_ref[...].reshape(INPUTS, INPUTS).astype(jnp.int32)
    row = lax.broadcasted_iota(jnp.int32, (HALF, HALF), 0)
    col = lax.broadcasted_iota(jnp.int32, (HALF, HALF), 1)
    low = jnp.where(col > row, codes[:HALF, :HALF], codes[HALF:, HALF:])
    code = jnp.concatenate([low, codes[:HALF, HALF:]], axis=1)
    row = lax.broadcasted_iota(jnp.int32, (HALF, INPUTS), 0)
    col = lax.broadcasted_iota(jnp.int32, (HALF, INPUTS), 1)
    target = jnp.where(code >= 0, code, -1 - code)
    sign_ref[...] = jnp.where(code >= 0, 1.0, -1.0).astype(F32)
    hi_ref[...] = lax.shift_right_logical(target, 7).astype(F32)
    lo_ref[...] = jnp.where(col != row, target & 127, -1).astype(F32)


def row_ids():
    sub = lax.broadcasted_iota(jnp.int32, (16, INPUTS), 0)
    return [(sub + r * 16).astype(F32).astype(BF16) for r in range(8)]


def one_hot(lo_ref, at, rows):
    one, zero = jnp.ones((), BF16), jnp.zeros((), BF16)
    lo = packed_row(lo_ref, at)
    return jnp.concatenate([jnp.where(lo == rows[r], one, zero) for r in range(8)], axis=0)


def count_pairs(first, last, hi_ref, lo_ref, count_ref):
    rows = row_ids()
    one, zero = jnp.ones((), BF16), jnp.zeros((), BF16)

    @pl.loop(first, last)
    def _(step):
        hots = [one_hot(lo_ref, step * CHUNK + n, rows) for n in range(CHUNK)]
        marks = [jnp.where(packed_row(hi_ref, step * CHUNK + n) == rows[0], one, zero) for n in range(CHUNK)]
        hot = jnp.concatenate(hots, axis=1)
        mark = jnp.concatenate(marks, axis=1)
        count_ref[...] += lax.dot_general(mark, hot, NT, preferred_element_type=F32)


def stack_pairs(x_ref, hi_ref, sign_ref, lo_ref, xf_ref, acc_ref):
    x = x_ref[...].reshape(INPUTS, 128)
    xf = x.astype(F32)
    xf_ref[0] = xf
    xf_ref[1] = jnp.concatenate([xf[:, 64:], -xf[:, :64]], axis=1)
    acc_ref[...] = jnp.zeros_like(acc_ref)
    lane = lax.broadcasted_iota(jnp.int32, (16, 128), 1)
    sub = lax.broadcasted_iota(jnp.int32, (16, 128), 0)
    pick = jnp.where(lane % 16 == sub, 1.0, 0.0).astype(BF16)
    lane_j = lax.broadcasted_iota(jnp.int32, (32, 128), 1)
    zero = jnp.zeros((), BF16)

    ids = row_ids()

    def produce(step):
        base = step * CHUNK
        left, right = [], []
        for n in range(CHUNK):
            for q in range(2):
                left.append(packed_row(xf_ref.at[q], base + n) * pick)
                right.append(packed_row(xf_ref.at[q], HALF + base + n) * pick)
        left = jnp.concatenate(left, axis=0)
        right = jnp.concatenate(right, axis=0)
        x = x_ref[...].reshape(INPUTS, 128)
        one = lax.dot_general(left, x, NT, preferred_element_type=F32)
        two = lax.dot_general(right, x[HALF:], NT, preferred_element_type=F32)
        data = []
        for n in range(CHUNK):
            at = slice(n * 32, n * 32 + 32)
            low = jnp.where(lane_j > base + n, one[at, :128], two[at, :])
            both = jnp.concatenate([low, one[at, 128:]], axis=1).astype(BF16)
            hi = packed_row(hi_ref, base + n)
            sign = packed_row(sign_ref, base + n)
            parts = []
            for b in range(NB):
                mine = hi == jnp.full((16, INPUTS), b, BF16)
                parts.append(jnp.where(mine, both[:16], zero))
                parts.append(jnp.where(mine, both[16:] * sign, zero))
            data.append(jnp.concatenate(parts, axis=0))
        hot = [one_hot(lo_ref, base + n, ids) for n in range(CHUNK)]
        return data, hot

    def product(data, hot):
        data = jnp.concatenate(data, axis=1)
        hot = jnp.concatenate(hot, axis=1)
        return lax.dot_general(hot, data, NT, preferred_element_type=F32)

    @pl.loop(0, HALF // CHUNK // UNROLL)
    def _(k):
        data, hot = [], []
        for u in range(UNROLL):
            d, h = produce(k * UNROLL + u)
            data += d
            hot += h
        acc_ref[...] += product(data, hot)


def messages(acc_ref, perm_ref, send_ref):
    turned = jnp.transpose(jnp.concatenate([acc_ref[...], jnp.zeros((128, 32), F32)], axis=1))
    sums = jnp.concatenate([turned[b * 32 : b * 32 + 32, :] for b in range(NB)], axis=1).astype(BF16)
    perm = perm_ref[...].reshape(FEEDS * 64, NB * 128)
    out = lax.dot_general(sums, perm, NT, preferred_element_type=F32)
    first = lax.broadcasted_iota(jnp.int32, (16, 128), 1) < 64
    for o in range(0, FEEDS, 2):
        real = out[:16, o * 64 : o * 64 + 128]
        imag = out[16:, o * 64 : o * 64 + 128]
        send_ref[o] = jnp.where(first, real, pltpu.roll(imag, 64, 1)).astype(BF16)
        send_ref[o + 1] = jnp.where(first, pltpu.roll(real, 64, 1), imag).astype(BF16)


def slot_scale(count_ref, perm):
    count = jnp.concatenate([count_ref[b : b + 1, :] for b in range(NB)], axis=1)
    high = jnp.floor(count * (1.0 / 256.0))
    digit = lax.broadcasted_iota(jnp.int32, (16, NB * 128), 0)
    digits = jnp.where(digit == 0, high, count - 256.0 * high).astype(BF16)
    got = lax.dot_general(perm, digits, NT, preferred_element_type=F32)
    return 1.0 / jnp.maximum(256.0 * got[:, 0:1] + got[:, 1:2], 1.0)


def finish(block, scale, out_ref):
    turned = jnp.transpose(block.astype(F32))
    for h in range(2):
        for q in range(2):
            mean = turned[q * 64 : q * 64 + CAP, h * 128 : h * 128 + 128] * scale[:CAP]
            out_ref[pl.ds(2 * h + q, CAP, stride=4), :] = mean


def far_first(axis):
    if axis == "feed":
        sizes, weights = (4, 2, 2), ((0, 3, 6, 3), (0, 6), (0, 1))
    else:
        sizes, weights = (4, 2), ((0, 3, 6, 3), (0, 3))
    offsets = [o for o in np.ndindex(*sizes) if any(o)]
    offsets.sort(key=lambda o: -sum(w[n] for w, n in zip(weights, o)))
    return sizes, offsets


def peers(axis):
    me = lax.axis_index(axis)
    sizes, offsets = far_first(axis)
    place, rest = [], me
    for size in reversed(sizes):
        place.insert(0, lax.rem(rest, size))
        rest = rest // size
    out = []
    for offset in offsets:
        peer = 0
        for size, at, step in zip(sizes, place, offset):
            peer = peer * size + lax.rem(at + step, size)
        out.append(peer)
    return out


def exchange(buffer, target, send_sem, recv_sem, axis):
    me = lax.axis_index(axis)
    others = peers(axis)
    for peer in others:
        pltpu.make_async_remote_copy(
            src_ref=buffer(peer),
            dst_ref=target.at[me],
            send_sem=send_sem,
            recv_sem=recv_sem,
            device_id={axis: peer},
            device_id_type=pl.DeviceIdType.MESH,
        ).start()
    whole = target.at[pl.ds(0, len(others))]
    every = pltpu.make_async_remote_copy(
        src_ref=whole,
        dst_ref=whole,
        send_sem=send_sem,
        recv_sem=recv_sem,
        device_id={axis: others[0]},
        device_id_type=pl.DeviceIdType.MESH,
    )
    return every.wait_recv, every.wait_send


def kernel(
    x_hbm, win_hbm, first_hbm, tw_hbm, second_hbm, code_hbm, owner_hbm, out_ref,
    x_ref, win_ref, first_ref, tw_ref, second_ref, owner_ref, raw_code,
    mixed_ref, wide_ref, wsend, wrecv, bsend, spec_ref, code_ref,
    hi_ref, sign_ref, lo_ref, perm_ref, count_ref,
    xf_ref, acc_ref, msend, mrecv,
    take_ref, known, local_sem, wss, wrs, css, crs, bss, brs, mss, mrs,
):
    feed = lax.axis_index("feed")
    chan = lax.axis_index("chan")
    z, yc = feed // 4, lax.rem(feed, 4)
    y, c = yc // 2, lax.rem(yc, 2)
    along_z = [{"feed": lax.rem(z + d, 4) * 4 + yc} for d in (2, 1, 3)]
    along_yc = [
        {"feed": z * 4 + lax.rem(y + e, 2) * 2 + lax.rem(c + d, 2)} for e, d in ((1, 1), (1, 0), (0, 1))
    ]
    barrier = pltpu.get_barrier_semaphore()
    for device in [{"chan": peer} for peer in peers("chan")] + along_z + along_yc:
        pl.semaphore_signal(barrier, inc=1, device_id=device, device_id_type=pl.DeviceIdType.MESH)
    loads = [
        pltpu.make_async_copy(a, b, local_sem.at[n])
        for n, (a, b) in enumerate([
            (x_hbm, x_ref), (win_hbm, win_ref), (first_hbm, first_ref), (tw_hbm, tw_ref),
            (second_hbm, second_ref), (code_hbm, raw_code), (owner_hbm, owner_ref),
        ])
    ]
    for load in loads:
        load.start()
    for load in loads:
        load.wait()
    wide = channelize(x_ref, win_ref, first_ref, tw_ref, second_ref, mixed_ref, wide_ref)
    wsend[...] = wide.reshape(GROUPS, 32, 128)
    code_ref[feed] = raw_code[...].astype(jnp.int16)
    permutation(owner_ref, perm_ref)
    take_ref[...] = regroup_matrix()
    pl.semaphore_wait(barrier, 13)
    for device in along_z:
        pl.semaphore_signal(known, inc=1, device_id=device, device_id_type=pl.DeviceIdType.MESH)
    w_arrived, w_sent = exchange(lambda d: wsend.at[d], wrecv, wss, wrs, "chan")
    wrecv[chan] = wsend[chan]
    pl.semaphore_wait(known, 3)
    c_arrived, c_sent = exchange(lambda d: code_ref.at[feed], code_ref, css, crs, "feed")
    w_arrived()
    regrouped = jnp.dot(take_ref[...], wrecv[...].reshape(256, 128), preferred_element_type=F32)
    bsend[...] = regrouped.astype(BF16).reshape(FEEDS, 16, 128)
    b_arrived, b_sent = exchange(lambda d: bsend.at[d], spec_ref, bss, brs, "feed")
    spec_ref[feed] = bsend[feed]
    c_arrived()
    unpack_codes(code_ref, hi_ref, sign_ref, lo_ref)
    count_ref[...] = jnp.zeros_like(count_ref)
    count_pairs(0, EARLY, hi_ref, lo_ref, count_ref)
    b_arrived()
    stack_pairs(spec_ref, hi_ref, sign_ref, lo_ref, xf_ref, acc_ref)
    messages(acc_ref, perm_ref, msend)
    m_arrived, m_sent = exchange(lambda d: msend.at[d], mrecv, mss, mrs, "feed")
    mrecv[feed] = msend[feed]
    count_pairs(EARLY, HALF // CHUNK, hi_ref, lo_ref, count_ref)
    scale = slot_scale(count_ref, perm_ref[feed])
    m_arrived()
    finish(mrecv[...].reshape(256, 128), scale, out_ref)
    w_sent()
    c_sent()
    b_sent()
    m_sent()


def per_device(raw_samples, stack_code, stack_owner):
    x = raw_samples.reshape(2, 704, 128).transpose(1, 0, 2).reshape(1408, 128)
    win = jnp.asarray(np.repeat(window_table(), 2, axis=1))
    owner = stack_owner
    rows = NB * 32
    dma = pltpu.SemaphoreType.DMA
    turned = pl.pallas_call(
        kernel,
        out_shape=pltpu.VMEM((4 * CAP, 128), F32),
        in_specs=[pl.BlockSpec(memory_space=pl.ANY)] * 7,
        out_specs=pl.BlockSpec(memory_space=pltpu.VMEM),
        scratch_shapes=[
            pltpu.VMEM((1408, 128), BF16),
            pltpu.VMEM((TAPS, 128, 128), F32),
            pltpu.VMEM((256, 128), BF16),
            pltpu.VMEM((2, 128, 128), F32),
            pltpu.VMEM((32, 256), BF16),
            pltpu.VMEM((STACKS,), jnp.int32),
            pltpu.VMEM((16, INPUTS), jnp.int32),
            pltpu.VMEM((1024, 256), BF16),
            pltpu.VMEM((256, 128), F32),
            pltpu.VMEM((GROUPS, 32, 128), BF16),
            pltpu.VMEM((GROUPS, 32, 128), BF16),
            pltpu.VMEM((FEEDS, 16, 128), BF16),
            pltpu.VMEM((FEEDS, 16, 128), BF16),
            pltpu.VMEM((FEEDS, 16, INPUTS), jnp.int16),
            pltpu.VMEM((HALF, INPUTS), F32),
            pltpu.VMEM((HALF, INPUTS), F32),
            pltpu.VMEM((HALF, INPUTS), F32),
            pltpu.VMEM((FEEDS, 64, NB * 128), BF16),
            pltpu.VMEM((16, 128), F32),
            pltpu.VMEM((2, INPUTS, 128), F32),
            pltpu.VMEM((128, rows), F32),
            pltpu.VMEM((FEEDS, 16, 128), BF16),
            pltpu.VMEM((FEEDS, 16, 128), BF16),
            pltpu.VMEM((256, 256), BF16),
            pltpu.SemaphoreType.REGULAR,
            dma((7,)),
            dma, dma, dma, dma, dma, dma, dma, dma,
        ],
        compiler_params=pltpu.CompilerParams(
            vmem_limit_bytes=60 << 20, collective_id=0, has_side_effects=True
        ),
    )(x, win, bf(first_matrix()), jnp.asarray(twiddle_tables()), bf(second_matrix()), stack_code, owner)
    return turned.reshape(CAP, 2, 2, 128).transpose(0, 2, 1, 3).reshape(CAP, 2, 256)


def solution(mesh):
    placed = (P(("feed", "chan"), None), P("feed", None), P())
    return jax.shard_map(
        per_device, mesh=mesh, in_specs=placed, out_specs=P("feed", None, "chan"), check_vma=False
    )
```

```python
import math

import numpy as np
import jax
import jax.numpy as jnp
from jax import lax
from jax.experimental import pallas as pl
from jax.experimental.pallas import tpu as pltpu
from jax.sharding import PartitionSpec as P

SPECTRA = 4
TAPS = 8
FA = 64
FB = 128
FRAME = 8192
STACKS = 382
CAP = 47
FEEDS = 16
GROUPS = 8
INPUTS = 256
HALF = 128
CHUNK = 16
UNROLL = 8
EARLY = 4
NB = 3
F32 = jnp.float32
BF16 = jnp.bfloat16
NT = (((1,), (1,)), ((), ()))


def window_table():
    length = TAPS * FRAME
    sample = np.arange(length, dtype=np.float64)
    centred = (sample - length / 2 + 0.5) / FRAME
    weights = np.sinc(centred) * (0.5 - 0.5 * np.cos(2.0 * np.pi * (sample + 0.5) / length))
    weights = weights * np.sqrt(FRAME / np.sum(weights * weights))
    return weights.reshape(TAPS, FA, FB).astype(np.float32)


def turns(left, right, modulus):
    return 2.0 * np.pi * (np.outer(left, right) % modulus) / modulus


def first_matrix():
    angles = turns(np.arange(FA), np.arange(FA), FA)
    parts = np.stack([np.cos(angles), -np.sin(angles)]).reshape(2, FA, 4, 16)
    out = np.zeros((2, 4, 2, 16, FA, 2), np.float32)
    for i in range(2):
        out[:, :, i, :, :, i] = parts.transpose(0, 2, 3, 1)
    return out.reshape(256, 128)


def twiddle_tables():
    angles = turns(np.arange(FA), np.arange(FB), FRAME).reshape(4, 1, 16, FB)
    angles = np.broadcast_to(angles, (4, 2, 16, FB)).reshape(128, FB)
    return np.stack([np.cos(angles), np.sin(angles)]).astype(np.float32)


def second_matrix():
    angles = turns(np.arange(32), np.arange(FB), FB)
    return np.concatenate([np.cos(angles), np.sin(angles)], axis=1).astype(np.float32)


def bf(table):
    return jnp.asarray(table).astype(BF16)


def channelize(x_ref, win_ref, first_ref, tw_ref, second_ref, mixed_ref, wide_ref):
    frames = []
    for t in range(SPECTRA):
        total = jnp.zeros((128, FB), F32)
        for p in range(TAPS):
            rows = x_ref[pl.ds((t + p) * 128, 128), :].astype(F32)
            total = total + win_ref[p] * rows
        frames.append(total.astype(BF16))
    frames = jnp.concatenate(frames, axis=1)
    section = jnp.dot(first_ref[...], frames, preferred_element_type=F32)
    cosine, sine = tw_ref[0], tw_ref[1]
    for t in range(SPECTRA):
        re = section[:128, t * FB : (t + 1) * FB]
        im = section[128:, t * FB : (t + 1) * FB]
        real = re * cosine + im * sine
        imag = im * cosine - re * sine
        minus = (-real).astype(BF16)
        real = real.astype(BF16)
        imag = imag.astype(BF16)
        for u in range(8):
            rows = slice(u * 16, u * 16 + 16)
            base = (u * 8 + t) * 16
            mixed_ref[base : base + 16, :FB] = real[rows]
            mixed_ref[base : base + 16, FB:] = imag[rows]
            base = (u * 8 + 4 + t) * 16
            mixed_ref[base : base + 16, :FB] = imag[rows]
            mixed_ref[base : base + 16, FB:] = minus[rows]
    out = lax.dot_general(second_ref[...], mixed_ref[...], NT, preferred_element_type=F32)
    out = out * (1.0 / math.sqrt(FRAME))
    for u in range(8):
        wide_ref[pl.ds(u, 32, stride=8), :] = out[:, u * 128 : (u + 1) * 128]
    return wide_ref[...].astype(BF16)


def regroup_matrix():
    row = lax.broadcasted_iota(jnp.int32, (256, 256), 0)
    col = lax.broadcasted_iota(jnp.int32, (256, 256), 1)
    source = ((row // 2) % 8) * 32 + (row // 16) * 2 + row % 2
    return jnp.where(col == source, 1.0, 0.0).astype(BF16)


def permutation(owner_ref, perm_ref):
    owner = jnp.concatenate([owner_ref[...].reshape(1, STACKS), jnp.full((1, NB * 128 - STACKS), -1, jnp.int32)], axis=1)
    tall = jnp.transpose(jnp.broadcast_to(owner, (128, NB * 128)).astype(F32))
    cols = []
    for b in range(NB):
        mine = owner[:, b * 128 : (b + 1) * 128].astype(F32)
        row = lax.broadcasted_iota(jnp.int32, (NB * 128, 128), 0)
        col = lax.broadcasted_iota(jnp.int32, (NB * 128, 128), 1) + b * 128
        same = jnp.where((tall == mine) & (row < col), 1.0, 0.0)
        cols.append(jnp.sum(same, axis=0, keepdims=True))
    rank = jnp.concatenate(cols, axis=1).astype(jnp.int32)
    place = jnp.where(owner >= 0, owner * 64 + rank, -1)

    @pl.loop(0, FEEDS)
    def _(o):
        slot = lax.broadcasted_iota(jnp.int32, (64, NB * 128), 0) + o * 64
        perm_ref[o] = jnp.where(slot == place, 1.0, 0.0).astype(BF16)


def packed_row(ref, at):
    return jnp.broadcast_to(ref[pl.ds(at, 1), :], (16, ref.shape[1])).astype(BF16)


def unpack_codes(code_ref, hi_ref, sign_ref, lo_ref):
    codes = code_ref[...].reshape(INPUTS, INPUTS).astype(jnp.int32)
    row = lax.broadcasted_iota(jnp.int32, (HALF, HALF), 0)
    col = lax.broadcasted_iota(jnp.int32, (HALF, HALF), 1)
    low = jnp.where(col > row, codes[:HALF, :HALF], codes[HALF:, HALF:])
    code = jnp.concatenate([low, codes[:HALF, HALF:]], axis=1)
    row = lax.broadcasted_iota(jnp.int32, (HALF, INPUTS), 0)
    col = lax.broadcasted_iota(jnp.int32, (HALF, INPUTS), 1)
    target = jnp.where(code >= 0, code, -1 - code)
    sign_ref[...] = jnp.where(code >= 0, 1.0, -1.0).astype(F32)
    hi_ref[...] = lax.shift_right_logical(target, 7).astype(F32)
    lo_ref[...] = jnp.where(col != row, target & 127, -1).astype(F32)


def row_ids():
    sub = lax.broadcasted_iota(jnp.int32, (16, INPUTS), 0)
    return [(sub + r * 16).astype(F32).astype(BF16) for r in range(8)]


def one_hot(lo_ref, at, rows):
    one, zero = jnp.ones((), BF16), jnp.zeros((), BF16)
    lo = packed_row(lo_ref, at)
    return jnp.concatenate([jnp.where(lo == rows[r], one, zero) for r in range(8)], axis=0)


def count_pairs(first, last, hi_ref, lo_ref, count_ref):
    rows = row_ids()
    one, zero = jnp.ones((), BF16), jnp.zeros((), BF16)

    @pl.loop(first, last)
    def _(step):
        hots = [one_hot(lo_ref, step * CHUNK + n, rows) for n in range(CHUNK)]
        marks = [jnp.where(packed_row(hi_ref, step * CHUNK + n) == rows[0], one, zero) for n in range(CHUNK)]
        hot = jnp.concatenate(hots, axis=1)
        mark = jnp.concatenate(marks, axis=1)
        count_ref[...] += lax.dot_general(mark, hot, NT, preferred_element_type=F32)


def stack_pairs(x_ref, hi_ref, sign_ref, lo_ref, xf_ref, acc_ref):
    x = x_ref[...].reshape(INPUTS, 128)
    xf = x.astype(F32)
    xf_ref[0] = xf
    xf_ref[1] = jnp.concatenate([xf[:, 64:], -xf[:, :64]], axis=1)
    acc_ref[...] = jnp.zeros_like(acc_ref)
    lane = lax.broadcasted_iota(jnp.int32, (16, 128), 1)
    sub = lax.broadcasted_iota(jnp.int32, (16, 128), 0)
    pick = jnp.where(lane % 16 == sub, 1.0, 0.0).astype(BF16)
    lane_j = lax.broadcasted_iota(jnp.int32, (32, 128), 1).astype(F32).astype(BF16)
    zero = jnp.zeros((), BF16)

    ids = row_ids()

    def produce(step):
        base = step * CHUNK
        left, right = [], []
        for n in range(CHUNK):
            for q in range(2):
                left.append(packed_row(xf_ref.at[q], base + n) * pick)
                right.append(packed_row(xf_ref.at[q], HALF + base + n) * pick)
        left = jnp.concatenate(left, axis=0)
        right = jnp.concatenate(right, axis=0)
        x = x_ref[...].reshape(INPUTS, 128)
        one = lax.dot_general(left, x, NT, preferred_element_type=F32)
        two = lax.dot_general(right, x[HALF:], NT, preferred_element_type=F32)
        data = []
        for n in range(CHUNK):
            at = slice(n * 32, n * 32 + 32)
            above = lane_j > (base + n).astype(F32).astype(BF16)
            low = jnp.where(above, one[at, :128].astype(BF16), two[at, :].astype(BF16))
            both = jnp.concatenate([low, one[at, 128:].astype(BF16)], axis=1)
            hi = packed_row(hi_ref, base + n)
            sign = packed_row(sign_ref, base + n)
            parts = []
            for b in range(NB):
                mine = hi == jnp.full((16, INPUTS), b, BF16)
                parts.append(jnp.where(mine, both[:16], zero))
                parts.append(jnp.where(mine, both[16:] * sign, zero))
            data.append(jnp.concatenate(parts, axis=0))
        hot = [one_hot(lo_ref, base + n, ids) for n in range(CHUNK)]
        return data, hot

    def product(data, hot):
        data = jnp.concatenate(data, axis=1)
        hot = jnp.concatenate(hot, axis=1)
        return lax.dot_general(hot, data, NT, preferred_element_type=F32)

    @pl.loop(0, HALF // CHUNK // UNROLL)
    def _(k):
        data, hot = [], []
        for u in range(UNROLL):
            d, h = produce(k * UNROLL + u)
            data += d
            hot += h
        acc_ref[...] += product(data, hot)


def messages(acc_ref, perm_ref, send_ref):
    turned = jnp.transpose(jnp.concatenate([acc_ref[...], jnp.zeros((128, 32), F32)], axis=1))
    sums = jnp.concatenate([turned[b * 32 : b * 32 + 32, :] for b in range(NB)], axis=1).astype(BF16)
    perm = perm_ref[...].reshape(FEEDS * 64, NB * 128)
    out = lax.dot_general(sums, perm, NT, preferred_element_type=F32)
    first = lax.broadcasted_iota(jnp.int32, (16, 128), 1) < 64
    for o in range(0, FEEDS, 2):
        real = out[:16, o * 64 : o * 64 + 128]
        imag = out[16:, o * 64 : o * 64 + 128]
        send_ref[o] = jnp.where(first, real, pltpu.roll(imag, 64, 1)).astype(BF16)
        send_ref[o + 1] = jnp.where(first, pltpu.roll(real, 64, 1), imag).astype(BF16)


def slot_scale(count_ref, perm):
    count = jnp.concatenate([count_ref[b : b + 1, :] for b in range(NB)], axis=1)
    high = jnp.floor(count * (1.0 / 256.0))
    digit = lax.broadcasted_iota(jnp.int32, (16, NB * 128), 0)
    digits = jnp.where(digit == 0, high, count - 256.0 * high).astype(BF16)
    got = lax.dot_general(perm, digits, NT, preferred_element_type=F32)
    return 1.0 / jnp.maximum(256.0 * got[:, 0:1] + got[:, 1:2], 1.0)


def finish(block, scale, out_ref):
    turned = jnp.transpose(block.astype(F32))
    for h in range(2):
        for q in range(2):
            mean = turned[q * 64 : q * 64 + CAP, h * 128 : h * 128 + 128] * scale[:CAP]
            out_ref[pl.ds(2 * h + q, CAP, stride=4), :] = mean


def far_first(axis):
    if axis == "feed":
        sizes, weights = (4, 2, 2), ((0, 3, 6, 3), (0, 6), (0, 1))
    else:
        sizes, weights = (4, 2), ((0, 3, 6, 3), (0, 3))
    offsets = [o for o in np.ndindex(*sizes) if any(o)]
    offsets.sort(key=lambda o: -sum(w[n] for w, n in zip(weights, o)))
    return sizes, offsets


def peers(axis):
    me = lax.axis_index(axis)
    sizes, offsets = far_first(axis)
    place, rest = [], me
    for size in reversed(sizes):
        place.insert(0, lax.rem(rest, size))
        rest = rest // size
    out = []
    for offset in offsets:
        peer = 0
        for size, at, step in zip(sizes, place, offset):
            peer = peer * size + lax.rem(at + step, size)
        out.append(peer)
    return out


def exchange(buffer, target, send_sem, recv_sem, axis):
    me = lax.axis_index(axis)
    others = peers(axis)
    for peer in others:
        pltpu.make_async_remote_copy(
            src_ref=buffer(peer),
            dst_ref=target.at[me],
            send_sem=send_sem,
            recv_sem=recv_sem,
            device_id={axis: peer},
            device_id_type=pl.DeviceIdType.MESH,
        ).start()
    whole = target.at[pl.ds(0, len(others))]
    every = pltpu.make_async_remote_copy(
        src_ref=whole,
        dst_ref=whole,
        send_sem=send_sem,
        recv_sem=recv_sem,
        device_id={axis: others[0]},
        device_id_type=pl.DeviceIdType.MESH,
    )
    return every.wait_recv, every.wait_send


def kernel(
    x_hbm, win_hbm, first_hbm, tw_hbm, second_hbm, code_hbm, owner_hbm, out_ref,
    x_ref, win_ref, first_ref, tw_ref, second_ref, owner_ref, raw_code,
    mixed_ref, wide_ref, wsend, wrecv, bsend, spec_ref, code_ref,
    hi_ref, sign_ref, lo_ref, perm_ref, count_ref,
    xf_ref, acc_ref, msend, mrecv,
    take_ref, known, local_sem, wss, wrs, css, crs, bss, brs, mss, mrs,
):
    feed = lax.axis_index("feed")
    chan = lax.axis_index("chan")
    z, yc = feed // 4, lax.rem(feed, 4)
    y, c = yc // 2, lax.rem(yc, 2)
    along_z = [{"feed": lax.rem(z + d, 4) * 4 + yc} for d in (2, 1, 3)]
    along_yc = [
        {"feed": z * 4 + lax.rem(y + e, 2) * 2 + lax.rem(c + d, 2)} for e, d in ((1, 1), (1, 0), (0, 1))
    ]
    barrier = pltpu.get_barrier_semaphore()
    for device in [{"chan": peer} for peer in peers("chan")] + along_z + along_yc:
        pl.semaphore_signal(barrier, inc=1, device_id=device, device_id_type=pl.DeviceIdType.MESH)
    loads = [
        pltpu.make_async_copy(a, b, local_sem.at[n])
        for n, (a, b) in enumerate([
            (x_hbm, x_ref), (win_hbm, win_ref), (first_hbm, first_ref), (tw_hbm, tw_ref),
            (second_hbm, second_ref), (code_hbm, raw_code), (owner_hbm, owner_ref),
        ])
    ]
    for load in loads:
        load.start()
    for load in loads:
        load.wait()
    wide = channelize(x_ref, win_ref, first_ref, tw_ref, second_ref, mixed_ref, wide_ref)
    wsend[...] = wide.reshape(GROUPS, 32, 128)
    code_ref[feed] = raw_code[...].astype(jnp.int16)
    permutation(owner_ref, perm_ref)
    take_ref[...] = regroup_matrix()
    pl.semaphore_wait(barrier, 13)
    for device in along_z:
        pl.semaphore_signal(known, inc=1, device_id=device, device_id_type=pl.DeviceIdType.MESH)
    w_arrived, w_sent = exchange(lambda d: wsend.at[d], wrecv, wss, wrs, "chan")
    wrecv[chan] = wsend[chan]
    pl.semaphore_wait(known, 3)
    c_arrived, c_sent = exchange(lambda d: code_ref.at[feed], code_ref, css, crs, "feed")
    w_arrived()
    regrouped = jnp.dot(take_ref[...], wrecv[...].reshape(256, 128), preferred_element_type=F32)
    bsend[...] = regrouped.astype(BF16).reshape(FEEDS, 16, 128)
    b_arrived, b_sent = exchange(lambda d: bsend.at[d], spec_ref, bss, brs, "feed")
    spec_ref[feed] = bsend[feed]
    c_arrived()
    unpack_codes(code_ref, hi_ref, sign_ref, lo_ref)
    count_ref[...] = jnp.zeros_like(count_ref)
    count_pairs(0, EARLY, hi_ref, lo_ref, count_ref)
    b_arrived()
    stack_pairs(spec_ref, hi_ref, sign_ref, lo_ref, xf_ref, acc_ref)
    messages(acc_ref, perm_ref, msend)
    m_arrived, m_sent = exchange(lambda d: msend.at[d], mrecv, mss, mrs, "feed")
    mrecv[feed] = msend[feed]
    count_pairs(EARLY, HALF // CHUNK, hi_ref, lo_ref, count_ref)
    scale = slot_scale(count_ref, perm_ref[feed])
    m_arrived()
    finish(mrecv[...].reshape(256, 128), scale, out_ref)
    w_sent()
    c_sent()
    b_sent()
    m_sent()


def per_device(raw_samples, stack_code, stack_owner):
    x = raw_samples.reshape(2, 704, 128).transpose(1, 0, 2).reshape(1408, 128)
    win = jnp.asarray(np.repeat(window_table(), 2, axis=1))
    owner = stack_owner
    rows = NB * 32
    dma = pltpu.SemaphoreType.DMA
    turned = pl.pallas_call(
        kernel,
        out_shape=pltpu.VMEM((4 * CAP, 128), F32),
        in_specs=[pl.BlockSpec(memory_space=pl.ANY)] * 7,
        out_specs=pl.BlockSpec(memory_space=pltpu.VMEM),
        scratch_shapes=[
            pltpu.VMEM((1408, 128), BF16),
            pltpu.VMEM((TAPS, 128, 128), F32),
            pltpu.VMEM((256, 128), BF16),
            pltpu.VMEM((2, 128, 128), F32),
            pltpu.VMEM((32, 256), BF16),
            pltpu.VMEM((STACKS,), jnp.int32),
            pltpu.VMEM((16, INPUTS), jnp.int32),
            pltpu.VMEM((1024, 256), BF16),
            pltpu.VMEM((256, 128), F32),
            pltpu.VMEM((GROUPS, 32, 128), BF16),
            pltpu.VMEM((GROUPS, 32, 128), BF16),
            pltpu.VMEM((FEEDS, 16, 128), BF16),
            pltpu.VMEM((FEEDS, 16, 128), BF16),
            pltpu.VMEM((FEEDS, 16, INPUTS), jnp.int16),
            pltpu.VMEM((HALF, INPUTS), F32),
            pltpu.VMEM((HALF, INPUTS), F32),
            pltpu.VMEM((HALF, INPUTS), F32),
            pltpu.VMEM((FEEDS, 64, NB * 128), BF16),
            pltpu.VMEM((16, 128), F32),
            pltpu.VMEM((2, INPUTS, 128), F32),
            pltpu.VMEM((128, rows), F32),
            pltpu.VMEM((FEEDS, 16, 128), BF16),
            pltpu.VMEM((FEEDS, 16, 128), BF16),
            pltpu.VMEM((256, 256), BF16),
            pltpu.SemaphoreType.REGULAR,
            dma((7,)),
            dma, dma, dma, dma, dma, dma, dma, dma,
        ],
        compiler_params=pltpu.CompilerParams(
            vmem_limit_bytes=60 << 20, collective_id=0, has_side_effects=True
        ),
    )(x, win, bf(first_matrix()), jnp.asarray(twiddle_tables()), bf(second_matrix()), stack_code, owner)
    return turned.reshape(CAP, 2, 2, 128).transpose(0, 2, 1, 3).reshape(CAP, 2, 256)


def solution(mesh):
    placed = (P(("feed", "chan"), None), P("feed", None), P())
    return jax.shard_map(
        per_device, mesh=mesh, in_specs=placed, out_specs=P("feed", None, "chan"), check_vma=False
    )
```

```python
import math

import numpy as np
import jax
import jax.numpy as jnp
from jax import lax
from jax.experimental import pallas as pl
from jax.experimental.pallas import tpu as pltpu
from jax.sharding import PartitionSpec as P

SPECTRA = 4
TAPS = 8
FA = 64
FB = 128
FRAME = 8192
STACKS = 382
CAP = 47
FEEDS = 16
GROUPS = 8
INPUTS = 256
HALF = 128
CHUNK = 16
UNROLL = 8
EARLY = 4
NB = 3
F32 = jnp.float32
BF16 = jnp.bfloat16
NT = (((1,), (1,)), ((), ()))


def window_table():
    length = TAPS * FRAME
    sample = np.arange(length, dtype=np.float64)
    centred = (sample - length / 2 + 0.5) / FRAME
    weights = np.sinc(centred) * (0.5 - 0.5 * np.cos(2.0 * np.pi * (sample + 0.5) / length))
    weights = weights * np.sqrt(FRAME / np.sum(weights * weights))
    return weights.reshape(TAPS, FA, FB).astype(np.float32)


def turns(left, right, modulus):
    return 2.0 * np.pi * (np.outer(left, right) % modulus) / modulus


def first_matrix():
    angles = turns(np.arange(FA), np.arange(FA), FA)
    parts = np.stack([np.cos(angles), -np.sin(angles)]).reshape(2, FA, 4, 16)
    out = np.zeros((2, 4, 2, 16, FA, 2), np.float32)
    for i in range(2):
        out[:, :, i, :, :, i] = parts.transpose(0, 2, 3, 1)
    return out.reshape(256, 128)


def twiddle_tables():
    angles = turns(np.arange(FA), np.arange(FB), FRAME).reshape(4, 1, 16, FB)
    angles = np.broadcast_to(angles, (4, 2, 16, FB)).reshape(128, FB)
    return np.stack([np.cos(angles), np.sin(angles)]).astype(np.float32)


def second_matrix():
    angles = turns(np.arange(32), np.arange(FB), FB)
    return np.concatenate([np.cos(angles), np.sin(angles)], axis=1).astype(np.float32)


def bf(table):
    return jnp.asarray(table).astype(BF16)


def channelize(x_ref, win_ref, first_ref, tw_ref, second_ref, mixed_ref, wide_ref):
    frames = []
    for t in range(SPECTRA):
        total = jnp.zeros((128, FB), F32)
        for p in range(TAPS):
            rows = x_ref[pl.ds((t + p) * 128, 128), :].astype(F32)
            total = total + win_ref[p] * rows
        frames.append(total.astype(BF16))
    frames = jnp.concatenate(frames, axis=1)
    section = jnp.dot(first_ref[...], frames, preferred_element_type=F32)
    cosine, sine = tw_ref[0], tw_ref[1]
    for t in range(SPECTRA):
        re = section[:128, t * FB : (t + 1) * FB]
        im = section[128:, t * FB : (t + 1) * FB]
        real = re * cosine + im * sine
        imag = im * cosine - re * sine
        minus = (-real).astype(BF16)
        real = real.astype(BF16)
        imag = imag.astype(BF16)
        for u in range(8):
            rows = slice(u * 16, u * 16 + 16)
            base = (u * 8 + t) * 16
            mixed_ref[base : base + 16, :FB] = real[rows]
            mixed_ref[base : base + 16, FB:] = imag[rows]
            base = (u * 8 + 4 + t) * 16
            mixed_ref[base : base + 16, :FB] = imag[rows]
            mixed_ref[base : base + 16, FB:] = minus[rows]
    out = lax.dot_general(second_ref[...], mixed_ref[...], NT, preferred_element_type=F32)
    out = out * (1.0 / math.sqrt(FRAME))
    for u in range(8):
        wide_ref[pl.ds(u, 32, stride=8), :] = out[:, u * 128 : (u + 1) * 128]
    return wide_ref[...].astype(BF16)


def regroup_matrix():
    row = lax.broadcasted_iota(jnp.int32, (256, 256), 0)
    col = lax.broadcasted_iota(jnp.int32, (256, 256), 1)
    source = ((row // 2) % 8) * 32 + (row // 16) * 2 + row % 2
    return jnp.where(col == source, 1.0, 0.0).astype(BF16)


def permutation(owner_ref, perm_ref):
    owner = jnp.concatenate([owner_ref[...].reshape(1, STACKS), jnp.full((1, NB * 128 - STACKS), -1, jnp.int32)], axis=1)
    tall = jnp.transpose(jnp.broadcast_to(owner, (128, NB * 128)).astype(F32))
    cols = []
    for b in range(NB):
        mine = owner[:, b * 128 : (b + 1) * 128].astype(F32)
        row = lax.broadcasted_iota(jnp.int32, (NB * 128, 128), 0)
        col = lax.broadcasted_iota(jnp.int32, (NB * 128, 128), 1) + b * 128
        same = jnp.where((tall == mine) & (row < col), 1.0, 0.0)
        cols.append(jnp.sum(same, axis=0, keepdims=True))
    rank = jnp.concatenate(cols, axis=1).astype(jnp.int32)
    place = jnp.where(owner >= 0, owner * 64 + rank, -1)

    @pl.loop(0, FEEDS)
    def _(o):
        slot = lax.broadcasted_iota(jnp.int32, (64, NB * 128), 0) + o * 64
        perm_ref[o] = jnp.where(slot == place, 1.0, 0.0).astype(BF16)


def packed_row(ref, at):
    return jnp.broadcast_to(ref[pl.ds(at, 1), :], (16, ref.shape[1])).astype(BF16)


def unpack_codes(code_ref, hi_ref, sign_ref, lo_ref):
    codes = code_ref[...].reshape(INPUTS, INPUTS).astype(jnp.int32)
    row = lax.broadcasted_iota(jnp.int32, (HALF, HALF), 0)
    col = lax.broadcasted_iota(jnp.int32, (HALF, HALF), 1)
    low = jnp.where(col > row, codes[:HALF, :HALF], codes[HALF:, HALF:])
    code = jnp.concatenate([low, codes[:HALF, HALF:]], axis=1)
    row = lax.broadcasted_iota(jnp.int32, (HALF, INPUTS), 0)
    col = lax.broadcasted_iota(jnp.int32, (HALF, INPUTS), 1)
    target = jnp.where(code >= 0, code, -1 - code)
    sign_ref[...] = jnp.where(code >= 0, 1.0, -1.0).astype(F32)
    hi_ref[...] = lax.shift_right_logical(target, 7).astype(F32)
    lo_ref[...] = jnp.where(col != row, target & 127, -1).astype(F32)


def row_ids():
    sub = lax.broadcasted_iota(jnp.int32, (16, INPUTS), 0)
    return [(sub + r * 16).astype(F32).astype(BF16) for r in range(8)]


def one_hot(lo_ref, at, rows):
    one, zero = jnp.ones((), BF16), jnp.zeros((), BF16)
    lo = packed_row(lo_ref, at)
    return jnp.concatenate([jnp.where(lo == rows[r], one, zero) for r in range(8)], axis=0)


def count_pairs(first, last, hi_ref, lo_ref, count_ref):
    rows = row_ids()
    one, zero = jnp.ones((), BF16), jnp.zeros((), BF16)

    @pl.loop(first, last)
    def _(step):
        hots = [one_hot(lo_ref, step * CHUNK + n, rows) for n in range(CHUNK)]
        marks = [jnp.where(packed_row(hi_ref, step * CHUNK + n) == rows[0], one, zero) for n in range(CHUNK)]
        hot = jnp.concatenate(hots, axis=1)
        mark = jnp.concatenate(marks, axis=1)
        count_ref[...] += lax.dot_general(mark, hot, NT, preferred_element_type=F32)


def stack_pairs(x_ref, hi_ref, sign_ref, lo_ref, xf_ref, acc_ref):
    x = x_ref[...].reshape(INPUTS, 128)
    xf = x.astype(F32)
    xf_ref[0] = xf
    xf_ref[1] = jnp.concatenate([xf[:, 64:], -xf[:, :64]], axis=1)
    acc_ref[...] = jnp.zeros_like(acc_ref)
    lane = lax.broadcasted_iota(jnp.int32, (16, 128), 1)
    sub = lax.broadcasted_iota(jnp.int32, (16, 128), 0)
    pick = jnp.where(lane % 16 == sub, 1.0, 0.0).astype(BF16)
    lane_j = lax.broadcasted_iota(jnp.int32, (32, 128), 1).astype(F32).astype(BF16)
    zero = jnp.zeros((), BF16)

    ids = row_ids()

    def produce(step):
        base = step * CHUNK
        left, right = [], []
        for n in range(CHUNK):
            for q in range(2):
                left.append(packed_row(xf_ref.at[q], base + n) * pick)
                right.append(packed_row(xf_ref.at[q], HALF + base + n) * pick)
        left = jnp.concatenate(left, axis=0)
        right = jnp.concatenate(right, axis=0)
        x = x_ref[...].reshape(INPUTS, 128)
        one = lax.dot_general(left, x, NT, preferred_element_type=F32)
        two = lax.dot_general(right, x[HALF:], NT, preferred_element_type=F32)
        data = []
        for n in range(CHUNK):
            at = slice(n * 32, n * 32 + 32)
            above = lane_j > (base + n).astype(F32).astype(BF16)
            low = jnp.where(above, one[at, :128].astype(BF16), two[at, :].astype(BF16))
            both = jnp.concatenate([low, one[at, 128:].astype(BF16)], axis=1)
            hi = packed_row(hi_ref, base + n)
            sign = packed_row(sign_ref, base + n)
            parts = []
            for b in range(NB):
                mine = hi == jnp.full((16, INPUTS), b, BF16)
                parts.append(jnp.where(mine, both[:16], zero))
                parts.append(jnp.where(mine, both[16:] * sign, zero))
            data.append(jnp.concatenate(parts, axis=0))
        hot = [one_hot(lo_ref, base + n, ids) for n in range(CHUNK)]
        return data, hot

    def product(data, hot):
        data = jnp.concatenate(data, axis=1)
        hot = jnp.concatenate(hot, axis=1)
        return lax.dot_general(hot, data, NT, preferred_element_type=F32)

    @pl.loop(0, HALF // CHUNK // UNROLL)
    def _(k):
        data, hot = [], []
        for u in range(UNROLL):
            d, h = produce(k * UNROLL + u)
            data += d
            hot += h
        acc_ref[...] += product(data, hot)


def messages(acc_ref, perm_ref, send_ref):
    turned = jnp.transpose(jnp.concatenate([acc_ref[...], jnp.zeros((128, 32), F32)], axis=1))
    sums = jnp.concatenate([turned[b * 32 : b * 32 + 32, :] for b in range(NB)], axis=1).astype(BF16)
    perm = perm_ref[...].reshape(FEEDS * 64, NB * 128)
    out = lax.dot_general(sums, perm, NT, preferred_element_type=F32)
    first = lax.broadcasted_iota(jnp.int32, (16, 128), 1) < 64
    for o in range(0, FEEDS, 2):
        real = out[:16, o * 64 : o * 64 + 128]
        imag = out[16:, o * 64 : o * 64 + 128]
        send_ref[o] = jnp.where(first, real, pltpu.roll(imag, 64, 1)).astype(BF16)
        send_ref[o + 1] = jnp.where(first, pltpu.roll(real, 64, 1), imag).astype(BF16)


def slot_scale(count_ref, perm):
    count = jnp.concatenate([count_ref[b : b + 1, :] for b in range(NB)], axis=1)
    high = jnp.floor(count * (1.0 / 256.0))
    digit = lax.broadcasted_iota(jnp.int32, (16, NB * 128), 0)
    digits = jnp.where(digit == 0, high, count - 256.0 * high).astype(BF16)
    got = lax.dot_general(perm, digits, NT, preferred_element_type=F32)
    return 1.0 / jnp.maximum(256.0 * got[:, 0:1] + got[:, 1:2], 1.0)


def finish(block, scale, out_ref):
    turned = jnp.transpose(block.astype(F32))
    for q in range(2):
        out_ref[:, q, :] = turned[q * 64 : q * 64 + CAP] * scale[:CAP]


def far_first(axis):
    if axis == "feed":
        sizes, weights = (4, 2, 2), ((0, 3, 6, 3), (0, 6), (0, 1))
    else:
        sizes, weights = (4, 2), ((0, 3, 6, 3), (0, 3))
    offsets = [o for o in np.ndindex(*sizes) if any(o)]
    offsets.sort(key=lambda o: -sum(w[n] for w, n in zip(weights, o)))
    return sizes, offsets


def peers(axis):
    me = lax.axis_index(axis)
    sizes, offsets = far_first(axis)
    place, rest = [], me
    for size in reversed(sizes):
        place.insert(0, lax.rem(rest, size))
        rest = rest // size
    out = []
    for offset in offsets:
        peer = 0
        for size, at, step in zip(sizes, place, offset):
            peer = peer * size + lax.rem(at + step, size)
        out.append(peer)
    return out


def exchange(buffer, target, send_sem, recv_sem, axis):
    me = lax.axis_index(axis)
    others = peers(axis)
    for peer in others:
        pltpu.make_async_remote_copy(
            src_ref=buffer(peer),
            dst_ref=target.at[me],
            send_sem=send_sem,
            recv_sem=recv_sem,
            device_id={axis: peer},
            device_id_type=pl.DeviceIdType.MESH,
        ).start()
    whole = target.at[pl.ds(0, len(others))]
    every = pltpu.make_async_remote_copy(
        src_ref=whole,
        dst_ref=whole,
        send_sem=send_sem,
        recv_sem=recv_sem,
        device_id={axis: others[0]},
        device_id_type=pl.DeviceIdType.MESH,
    )
    return every.wait_recv, every.wait_send


def kernel(
    x_hbm, win_hbm, first_hbm, tw_hbm, second_hbm, code_hbm, owner_hbm, out_ref,
    x_ref, win_ref, first_ref, tw_ref, second_ref, owner_ref, raw_code,
    mixed_ref, wide_ref, wsend, wrecv, bsend, spec_ref, code_ref,
    hi_ref, sign_ref, lo_ref, perm_ref, count_ref,
    xf_ref, acc_ref, msend, mrecv,
    take_ref, known, local_sem, wss, wrs, css, crs, bss, brs, mss, mrs,
):
    feed = lax.axis_index("feed")
    chan = lax.axis_index("chan")
    z, yc = feed // 4, lax.rem(feed, 4)
    y, c = yc // 2, lax.rem(yc, 2)
    along_z = [{"feed": lax.rem(z + d, 4) * 4 + yc} for d in (2, 1, 3)]
    along_yc = [
        {"feed": z * 4 + lax.rem(y + e, 2) * 2 + lax.rem(c + d, 2)} for e, d in ((1, 1), (1, 0), (0, 1))
    ]
    barrier = pltpu.get_barrier_semaphore()
    for device in [{"chan": peer} for peer in peers("chan")] + along_z + along_yc:
        pl.semaphore_signal(barrier, inc=1, device_id=device, device_id_type=pl.DeviceIdType.MESH)
    loads = [
        pltpu.make_async_copy(a, b, local_sem.at[n])
        for n, (a, b) in enumerate([
            (x_hbm, x_ref), (win_hbm, win_ref), (first_hbm, first_ref), (tw_hbm, tw_ref),
            (second_hbm, second_ref), (code_hbm, raw_code), (owner_hbm, owner_ref),
        ])
    ]
    for load in loads:
        load.start()
    for load in loads:
        load.wait()
    wide = channelize(x_ref, win_ref, first_ref, tw_ref, second_ref, mixed_ref, wide_ref)
    wsend[...] = wide.reshape(GROUPS, 32, 128)
    code_ref[feed] = raw_code[...].astype(jnp.int16)
    permutation(owner_ref, perm_ref)
    take_ref[...] = regroup_matrix()
    pl.semaphore_wait(barrier, 13)
    for device in along_z:
        pl.semaphore_signal(known, inc=1, device_id=device, device_id_type=pl.DeviceIdType.MESH)
    w_arrived, w_sent = exchange(lambda d: wsend.at[d], wrecv, wss, wrs, "chan")
    wrecv[chan] = wsend[chan]
    pl.semaphore_wait(known, 3)
    c_arrived, c_sent = exchange(lambda d: code_ref.at[feed], code_ref, css, crs, "feed")
    w_arrived()
    regrouped = jnp.dot(take_ref[...], wrecv[...].reshape(256, 128), preferred_element_type=F32)
    bsend[...] = regrouped.astype(BF16).reshape(FEEDS, 16, 128)
    b_arrived, b_sent = exchange(lambda d: bsend.at[d], spec_ref, bss, brs, "feed")
    spec_ref[feed] = bsend[feed]
    c_arrived()
    unpack_codes(code_ref, hi_ref, sign_ref, lo_ref)
    count_ref[...] = jnp.zeros_like(count_ref)
    count_pairs(0, EARLY, hi_ref, lo_ref, count_ref)
    b_arrived()
    stack_pairs(spec_ref, hi_ref, sign_ref, lo_ref, xf_ref, acc_ref)
    messages(acc_ref, perm_ref, msend)
    m_arrived, m_sent = exchange(lambda d: msend.at[d], mrecv, mss, mrs, "feed")
    mrecv[feed] = msend[feed]
    count_pairs(EARLY, HALF // CHUNK, hi_ref, lo_ref, count_ref)
    scale = slot_scale(count_ref, perm_ref[feed])
    m_arrived()
    finish(mrecv[...].reshape(256, 128), scale, out_ref)
    w_sent()
    c_sent()
    b_sent()
    m_sent()


def per_device(raw_samples, stack_code, stack_owner):
    x = raw_samples.reshape(2, 704, 128).transpose(1, 0, 2).reshape(1408, 128)
    win = jnp.asarray(np.repeat(window_table(), 2, axis=1))
    owner = stack_owner
    rows = NB * 32
    dma = pltpu.SemaphoreType.DMA
    turned = pl.pallas_call(
        kernel,
        out_shape=pltpu.VMEM((CAP, 2, 256), F32),
        in_specs=[pl.BlockSpec(memory_space=pl.ANY)] * 7,
        out_specs=pl.BlockSpec(memory_space=pltpu.VMEM),
        scratch_shapes=[
            pltpu.VMEM((1408, 128), BF16),
            pltpu.VMEM((TAPS, 128, 128), F32),
            pltpu.VMEM((256, 128), BF16),
            pltpu.VMEM((2, 128, 128), F32),
            pltpu.VMEM((32, 256), BF16),
            pltpu.VMEM((STACKS,), jnp.int32),
            pltpu.VMEM((16, INPUTS), jnp.int32),
            pltpu.VMEM((1024, 256), BF16),
            pltpu.VMEM((256, 128), F32),
            pltpu.VMEM((GROUPS, 32, 128), BF16),
            pltpu.VMEM((GROUPS, 32, 128), BF16),
            pltpu.VMEM((FEEDS, 16, 128), BF16),
            pltpu.VMEM((FEEDS, 16, 128), BF16),
            pltpu.VMEM((FEEDS, 16, INPUTS), jnp.int16),
            pltpu.VMEM((HALF, INPUTS), F32),
            pltpu.VMEM((HALF, INPUTS), F32),
            pltpu.VMEM((HALF, INPUTS), F32),
            pltpu.VMEM((FEEDS, 64, NB * 128), BF16),
            pltpu.VMEM((16, 128), F32),
            pltpu.VMEM((2, INPUTS, 128), F32),
            pltpu.VMEM((128, rows), F32),
            pltpu.VMEM((FEEDS, 16, 128), BF16),
            pltpu.VMEM((FEEDS, 16, 128), BF16),
            pltpu.VMEM((256, 256), BF16),
            pltpu.SemaphoreType.REGULAR,
            dma((7,)),
            dma, dma, dma, dma, dma, dma, dma, dma,
        ],
        compiler_params=pltpu.CompilerParams(
            vmem_limit_bytes=60 << 20, collective_id=0, has_side_effects=True
        ),
    )(x, win, bf(first_matrix()), jnp.asarray(twiddle_tables()), bf(second_matrix()), stack_code, owner)
    return turned


def solution(mesh):
    placed = (P(("feed", "chan"), None), P("feed", None), P())
    return jax.shard_map(
        per_device, mesh=mesh, in_specs=placed, out_specs=P("feed", None, "chan"), check_vma=False
    )
```
